768 devices in a mesh: lat: 32 (over y, x), lon: 24 (over z, core).
Axes of the slice: x: 4, y: 8, z: 12, core: 2. Of those that a mesh axis runs over, the one named last changes fastest.
Arguments:
- fields: bfloat16 [768, 3072, 128], P('lat', 'lon'), may hold values from -6 to 6
- req_block: int32 [32, 24, 3, 1280], P('lat', 'lon'), may hold values from 0 to 191
- req_stencil: int32 [32, 24, 3, 4, 1280], P('lat', 'lon'), may hold values from 0 to 15
- req_frac: int32 [32, 24, 3, 2, 1280], P('lat', 'lon'), may hold values from 0 to 15
- req_count: int32 [32, 24, 3], P('lat', 'lon'), may hold values from 597 to 1280, as said below
- legendre: bfloat16 [1536, 768, 768], P(('lon', 'lat')), may hold values from -0.21875 to 0.21875
Outputs:
- spectral: float32 [1536, 768, 128], P(('lon', 'lat'))
The draws below stay inside these ranges and needn't reach their ends.
Inputs may be any that keep to these rules, and one draw needn't show every extreme that they name: `req_count`: the three counts of a tile sum to 3072; positions j at or beyond a slot's count are unused. In every latitude band some tile receives 1280 points from each of the three tiles whose slots reach it, and every tile fills one slot to 1280.
All inputs are finite; a program needn't handle non-finite values.
Results may differ from the reference program's by a relative error of at most 0.0048.
Values may be sent and summed in bfloat16 or wider, within the bound.
A program may use at most 32 MiB of HBM per device.

```python
import math
import jax
import jax.numpy as jnp
from jax import lax

CHANNELS = 128
LAT_DEV = 24
LON_DEV = 128
KF = 1536
NN = 768
BLK = 16
FRAC = 16
COLS = 3072
CAP = 1280
NLAT = 768
NLON = 3072
N_LAT = 32
N_LON = 24


def draw_req_count(key, part):
    key_hot = jax.random.fold_in(key, 11)
    key_jet = jax.random.fold_in(key, 23)
    key_share = jax.random.fold_in(key, 37)
    hot_sector = jax.random.randint(key_hot, (N_LAT, 1), 0, N_LON)
    source = jnp.arange(N_LON, dtype=jnp.int32)[None, :]
    toward_hot = (hot_sector - source + 1) % N_LON
    jet_slot = jax.random.randint(key_jet, (N_LAT, N_LON), 0, 3)
    full_slot = jnp.where(toward_hot <= 2, toward_hot, jet_slot)
    slot_index = jnp.arange(3, dtype=jnp.int32)[None, None, :]
    is_full = slot_index == full_slot[:, :, None]
    weights = jax.random.randint(key_share, (N_LAT, N_LON, 3), 2, 5)
    weights = jnp.where(is_full, 0, weights)
    remaining = COLS - CAP
    shares = remaining * weights // jnp.sum(weights, axis=2, keepdims=True)
    leftover = remaining - jnp.sum(shares, axis=2, keepdims=True)
    first_other = jnp.where(full_slot == 0, 1, 0)
    shares = shares + jnp.where(slot_index == first_other[:, :, None], leftover, 0)
    return jnp.where(is_full, CAP, shares).astype(jnp.int32)


def set_ends(array, stream_key, smallest, top_value):
    spot = [jax.random.randint(jax.random.fold_in(stream_key, axis), (), 0, length) for axis, length in enumerate(array.shape)]
    widest = array.shape.index(max(array.shape))
    beside = spot[:widest] + [(spot[widest] + 1) % array.shape[widest]] + spot[widest + 1:]
    return array.at[tuple(spot)].set(smallest).at[tuple(beside)].set(top_value)


def shard_levels(rng, shape, cuts, least, high):
    loudness = 1.0
    for position, parts in cuts:
        steps = jax.random.uniform(jax.random.fold_in(jax.random.fold_in(rng, 6), position), (parts,), jnp.float32, least / len(cuts), high / len(cuts))
        loudness = loudness * jnp.repeat(jnp.exp(steps), shape[position] // parts).reshape((-1,) + (1,) * (len(shape) - 1 - position))
    return loudness


def noise(own_key, dims, scale, bound, split=(), held_as=jnp.bfloat16):
    entries = scale * jax.random.normal(own_key, dims, jnp.float32)
    if split:
        entries = entries * shard_levels(own_key, dims, split, -0.22, 0.18)
    return jnp.clip(entries, -bound, bound).astype(held_as)


def setup_inputs(seed: int = 0) -> dict:
    keys = jax.random.split(jax.random.key(seed), 7)
    fields = noise(keys[0], (NLAT, NLON, CHANNELS), 1.0, 6.0, ((0, 32), (1, 24)))
    req_block = set_ends(jax.random.randint(keys[1], (NLAT // LAT_DEV, NLON // LON_DEV, 3, CAP), 0, COLS // BLK), jax.random.fold_in(keys[1], 1), 0, (COLS // BLK) - 1).astype(jnp.int32)
    req_stencil = set_ends(jax.random.randint(keys[2], (NLAT // LAT_DEV, NLON // LON_DEV, 3, 4, CAP), 0, BLK), jax.random.fold_in(keys[2], 1), 0, BLK - 1).astype(jnp.int32)
    req_frac = set_ends(jax.random.randint(keys[3], (NLAT // LAT_DEV, NLON // LON_DEV, 3, 2, CAP), 0, FRAC), jax.random.fold_in(keys[3], 1), 0, FRAC - 1).astype(jnp.int32)
    req_count = draw_req_count(jax.random.fold_in(keys[6], 71), 0)
    legendre = noise(keys[5], (KF, NLAT, NN), NLAT ** -0.5, 0.21875, ((0, 768),))
    return {"fields": fields, "req_block": req_block, "req_stencil": req_stencil, "req_frac": req_frac, "req_count": req_count, "legendre": legendre}


def hartley_table(lon_total):
    wave_index = jnp.arange(KF, dtype=jnp.int32)
    lon_index = jnp.arange(lon_total, dtype=jnp.int32)
    phase_index = wave_index[:, None] * lon_index[None, :] % lon_total
    phase_angle = 2.0 * math.pi / lon_total * phase_index.astype(jnp.float32)
    return ((jnp.cos(phase_angle) + jnp.sin(phase_angle)) / math.sqrt(lon_total)).astype(jnp.bfloat16)

def interpolate(own_tile, packed):
    cell_rows = (packed[0][None, :] * BLK + packed[1:5]).astype(jnp.int32)
    picked = jnp.take(own_tile, cell_rows.reshape(-1), axis=0).astype(jnp.float32)
    picked = picked.reshape(4, cell_rows.shape[1], own_tile.shape[1])
    frac_lat = (packed[5].astype(jnp.float32) + 0.5) / FRAC
    frac_lon = (packed[6].astype(jnp.float32) + 0.5) / FRAC
    weights = jnp.stack([(1.0 - frac_lat) * (1.0 - frac_lon), frac_lat * (1.0 - frac_lon), (1.0 - frac_lat) * frac_lon, frac_lat * frac_lon])
    return lax.optimization_barrier(jnp.sum(weights[:, :, None] * picked, axis=0)).astype(jnp.bfloat16)

def place_columns(values, counts):
    slot_ends = jnp.cumsum(counts).astype(jnp.int32)
    starts = slot_ends - counts
    column = jnp.arange(COLS, dtype=jnp.int32)
    slot_index = lax.optimization_barrier(jnp.sum((slot_ends[None, :] <= column[:, None]).astype(jnp.int32), axis=1))
    onehot = slot_index[:, None] == jnp.arange(3, dtype=jnp.int32)[None, :]
    offset = column - lax.optimization_barrier(jnp.sum(jnp.where(onehot, starts[None, :], 0), axis=1)).astype(jnp.int32)
    flat_index = (slot_index * values.shape[1] + offset).astype(jnp.int32)
    return jnp.take(values.reshape(-1, values.shape[-1]), flat_index, axis=0)

def reference(fields, req_block, req_stencil, req_frac, req_count, legendre):
    lon_total = LON_DEV * N_LON
    lat_total = LAT_DEV * N_LAT
    all_tiles = fields.reshape(N_LAT, LAT_DEV, N_LON, LON_DEV, CHANNELS).transpose(0, 2, 1, 3, 4)
    all_tiles = all_tiles.reshape(N_LAT, N_LON, COLS, CHANNELS)
    packed = jnp.concatenate([req_block[:, :, :, None, :], req_stencil, req_frac], axis=3)
    hartley = hartley_table(lon_total).astype(jnp.float32)

    def one_band(inputs):
        band_tiles, band_packed, band_count = inputs

        def one_source(source):
            slot_values = []
            for slot_index in range(3):
                owner = (source + slot_index - 1) % N_LON
                slot_values.append(interpolate(band_tiles[owner], band_packed[source, slot_index]))
            return place_columns(jnp.stack(slot_values), band_count[source])
        departed = jax.vmap(one_source)(jnp.arange(N_LON, dtype=jnp.int32))
        band_grid = departed.reshape(N_LON, LAT_DEV, LON_DEV, CHANNELS).transpose(1, 0, 2, 3)
        band_grid = band_grid.reshape(LAT_DEV, lon_total, CHANNELS).astype(jnp.float32)
        fourier = jnp.einsum('kx,yxc->ykc', hartley, band_grid)
        return fourier.astype(jnp.bfloat16)
    fourier = lax.map(one_band, (all_tiles, packed, req_count)).reshape(lat_total, KF, CHANNELS)
    blocks = KF // 64
    leg_blocks = legendre.reshape(blocks, 64, lat_total, NN)
    four_blocks = fourier.reshape(lat_total, blocks, 64, CHANNELS).transpose(1, 0, 2, 3)

    def project(inputs):
        leg_block, four_block = inputs
        return jnp.einsum('kyn,ykc->knc', leg_block.astype(jnp.float32), four_block.astype(jnp.float32))
    projected = lax.map(project, (leg_blocks, four_blocks)).reshape(KF, NN, CHANNELS)
    degree = jnp.arange(NN, dtype=jnp.float32)
    factor = 1.0 / (1.0 + 4.0 * degree * (degree + 1.0) / (NN * (NN + 1)))
    return projected * factor[None, :, None]
```

```python
import functools
import math

import jax
import jax.numpy as jnp
import numpy as np
from jax import lax
from jax.experimental import pallas as pl
from jax.experimental.pallas import tpu as pltpu
from jax.sharding import PartitionSpec as P

KF = 1536
NN = 768
BLK = 16
FRAC = 16
COLS = 3072
CAP = 1280
NLON = 3072
BLOCKS = COLS // BLK
FINE = 48


def small_tables():
    unit = 2.0 * math.pi / NLON
    fine = np.arange(FINE, dtype=np.int64)[:, None]
    lane = np.arange(128, dtype=np.int64)[None, :]
    scale = 1.0 / math.sqrt(NLON)
    near = unit * (fine * lane % NLON)
    plus = (np.cos(near) + np.sin(near)) * scale
    minus = (np.cos(near) - np.sin(near)) * scale
    far = unit * (fine * lane * 128 % NLON)
    coarse = unit * (np.arange(KF // FINE, dtype=np.int64)[:, None] * FINE * lane % NLON)
    tables = [plus, minus, np.cos(far), np.sin(far), np.cos(coarse), np.sin(coarse)]
    return [np.asarray(t, dtype=np.float32) for t in tables]


def cell_requests(req_block, req_stencil, req_frac, counts):
    packed = (
        (req_block << 24)
        | (req_stencil[:, 0] << 20)
        | (req_stencil[:, 1] << 16)
        | (req_stencil[:, 2] << 12)
        | (req_stencil[:, 3] << 8)
        | (req_frac[:, 0] << 4)
        | req_frac[:, 1]
    )
    first = counts[0]
    second = first + counts[1]
    cells = jnp.zeros((COLS + CAP,), jnp.int32)
    cells = lax.dynamic_update_slice(cells, packed[0], (0,))
    cells = lax.dynamic_update_slice(cells, packed[1], (first,))
    cells = lax.dynamic_update_slice(cells, packed[2], (second,))
    return cells[:COLS].reshape(COLS // 128, 128), jnp.stack([first, second])


def decode(ends_ref, cells_ref, onehot_ref, weight_ref):
    rows = cells_ref.shape[0]
    columns = jnp.concatenate(
        [cells_ref[...], jnp.zeros((128 - rows, 128), jnp.int32)], axis=0
    ).T
    lane = lax.broadcasted_iota(jnp.int32, (128, 128), 1)
    sub = lax.broadcasted_iota(jnp.int32, (128, 128), 0)
    for row in range(rows):
        word = jnp.broadcast_to(columns[:, row : row + 1], (128, 128))
        block = lax.shift_right_logical(word, 24)
        edge = ends_ref[0] if row < rows // 2 else ends_ref[1]
        block = block + jnp.where(sub + row * 128 >= edge, BLOCKS, 0)
        here = pl.ds(row * 128, 128)
        for part in range(3):
            onehot_ref[here, part * 128 : (part + 1) * 128] = jnp.where(
                block == lane + part * 128, 1.0, 0.0
            ).astype(jnp.bfloat16)
        frac_lat = ((lax.shift_right_logical(word, 4) & 15).astype(jnp.float32) + 0.5) / FRAC
        frac_lon = ((word & 15).astype(jnp.float32) + 0.5) / FRAC
        corner = (
            (1.0 - frac_lat) * (1.0 - frac_lon),
            frac_lat * (1.0 - frac_lon),
            (1.0 - frac_lat) * frac_lon,
            frac_lat * frac_lon,
        )
        weight = jnp.zeros((128, 128), jnp.float32)
        for k in range(4):
            spot = lax.shift_right_logical(word, 20 - 4 * k) & 15
            weight = weight + jnp.where(spot == lane, corner[k], 0.0)
        weight_ref[here, :] = weight


def interpolate_kernel(ends_ref, cells_ref, left_ref, own_ref, right_ref, out_ref, tiles, onehot, weight):
    tiles[:BLOCKS, :] = left_ref[...]
    tiles[BLOCKS : 2 * BLOCKS, :] = own_ref[...]
    tiles[2 * BLOCKS :, :] = right_ref[...]
    decode(ends_ref, cells_ref, onehot, weight)
    step = 512
    for half in range(2):
        low = half * BLOCKS
        for part in range(COLS // 2 // step):
            here = pl.ds(half * (COLS // 2) + part * step, step)
            total = jnp.zeros((step, 128), jnp.float32)
            for pair in range(BLK // 2):
                got = jnp.dot(
                    onehot[here, :],
                    tiles[low : low + 2 * BLOCKS, pair * 256 : (pair + 1) * 256],
                    preferred_element_type=jnp.float32,
                )
                scale = weight[here, :]
                total = total + scale[:, 2 * pair : 2 * pair + 1] * got[:, :128]
                total = total + scale[:, 2 * pair + 1 : 2 * pair + 2] * got[:, 128:]
            out_ref[here, :] = total.astype(jnp.bfloat16)


def interpolate(ends, cells, left, own, right):
    vmem = pl.BlockSpec(memory_space=pltpu.VMEM)
    return pl.pallas_call(
        interpolate_kernel,
        out_shape=jax.ShapeDtypeStruct((COLS, 128), jnp.bfloat16),
        in_specs=[pl.BlockSpec(memory_space=pltpu.SMEM), vmem, vmem, vmem, vmem],
        out_specs=vmem,
        scratch_shapes=[
            pltpu.VMEM((3 * BLOCKS, BLK * 128), jnp.bfloat16),
            pltpu.VMEM((COLS, 2 * BLOCKS), jnp.bfloat16),
            pltpu.VMEM((COLS, 128), jnp.float32),
        ],
        compiler_params=pltpu.CompilerParams(vmem_limit_bytes=40 << 20),
        name="interpolate",
    )(ends, cells, left, own, right)


def fill_table(small, plus, minus, table):
    near_plus, near_minus, far_cos, far_sin, coarse_cos, coarse_sin = small
    for sector in range(NLON // 128):
        here = pl.ds(sector * 128, 128)
        turn_cos = far_cos[:, sector : sector + 1]
        turn_sin = far_sin[:, sector : sector + 1]
        plus[:, here] = turn_cos * near_plus[...] + turn_sin * near_minus[...]
        minus[:, here] = turn_cos * near_minus[...] - turn_sin * near_plus[...]

    def body(step, carry):
        cos = coarse_cos[pl.ds(step, 1), :]
        sin = coarse_sin[pl.ds(step, 1), :]
        rows = pl.ds(pl.multiple_of(step * FINE, FINE), FINE)
        for sector in range(NLON // 128):
            here = slice(sector * 128, (sector + 1) * 128)
            table[sector // 2, rows, (sector % 2) * 128 : (sector % 2 + 1) * 128] = (
                cos * plus[:, here] + sin * minus[:, here]
            ).astype(jnp.bfloat16)
        return carry

    lax.fori_loop(0, KF // FINE, body, 0)


def hartley_kernel(rows_ref, *refs):
    small, out_ref, plus, minus, table = refs[:6], refs[6], refs[7], refs[8], refs[9]
    fill_table(small, plus, minus, table)
    step = 512
    for part in range(KF // step):
        total = jnp.zeros((step, 128), jnp.float32)
        for pair in range(NLON // 256):
            total = total + jnp.dot(
                table[pair, part * step : (part + 1) * step, :],
                rows_ref[pair * 256 : (pair + 1) * 256, :],
                preferred_element_type=jnp.float32,
            )
        out_ref[part * step : (part + 1) * step, :] = total.astype(jnp.bfloat16)


def hartley(rows):
    vmem = pl.BlockSpec(memory_space=pltpu.VMEM)
    return pl.pallas_call(
        hartley_kernel,
        out_shape=jax.ShapeDtypeStruct((KF, 128), jnp.bfloat16),
        in_specs=[vmem] * 7,
        out_specs=vmem,
        scratch_shapes=[
            pltpu.VMEM((FINE, NLON), jnp.float32),
            pltpu.VMEM((FINE, NLON), jnp.float32),
            pltpu.VMEM((NLON // 256, KF, 256), jnp.bfloat16),
        ],
        compiler_params=pltpu.CompilerParams(vmem_limit_bytes=40 << 20),
        name="hartley",
    )(rows, *small_tables())


def local(fields, req_block, req_stencil, req_frac, req_count, legendre):
    lon = lax.axis_size("lon")
    lat = lax.axis_size("lat")
    tile = fields.reshape(BLOCKS, BLK * 128)
    left = lax.ppermute(tile, "lon", [(i, (i + 1) % lon) for i in range(lon)])
    right = lax.ppermute(tile, "lon", [((i + 1) % lon, i) for i in range(lon)])
    cells, ends = cell_requests(req_block[0, 0], req_stencil[0, 0], req_frac[0, 0], req_count[0, 0])
    departed = interpolate(ends, cells, left, tile, right)
    rows = lax.all_to_all(departed.reshape(24, 128, 128), "lon", split_axis=0, concat_axis=0, tiled=True)
    spectra = hartley(rows.reshape(NLON, 128))
    fourier = lax.all_to_all(
        spectra.reshape(lon, KF // lon, 128), "lon", split_axis=0, concat_axis=0, tiled=True
    )
    gathered = lax.all_to_all(fourier, "lat", split_axis=1, concat_axis=0, tiled=True)
    projected = jnp.einsum("kyn,ykc->knc", legendre, gathered, preferred_element_type=jnp.float32)
    degree = jnp.arange(NN, dtype=jnp.float32)
    factor = 1.0 / (1.0 + 4.0 * degree * (degree + 1.0) / (NN * (NN + 1)))
    return projected * factor[None, :, None]


def solution(mesh):
    return jax.shard_map(
        local,
        mesh=mesh,
        in_specs=(
            P("lat", "lon", None),
            P("lat", "lon", None, None),
            P("lat", "lon", None, None, None),
            P("lat", "lon", None, None, None),
            P("lat", "lon", None),
            P(("lon", "lat"), None, None),
        ),
        out_specs=P(("lon", "lat"), None, None),
        check_vma=False,
    )
```

```python
import functools
import math

import jax
import jax.numpy as jnp
import numpy as np
from jax import lax
from jax.experimental import pallas as pl
from jax.experimental.pallas import tpu as pltpu
from jax.sharding import PartitionSpec as P

KF = 1536
NN = 768
BLK = 16
FRAC = 16
COLS = 3072
CAP = 1280
NLON = 3072
BLOCKS = COLS // BLK
FINE = 48
CHUNK = 4
MESH = pl.DeviceIdType.MESH


def small_tables():
    unit = 2.0 * math.pi / NLON
    fine = np.arange(FINE, dtype=np.int64)[:, None]
    lane = np.arange(128, dtype=np.int64)[None, :]
    scale = 1.0 / math.sqrt(NLON)
    near = unit * (fine * lane % NLON)
    plus = (np.cos(near) + np.sin(near)) * scale
    minus = (np.cos(near) - np.sin(near)) * scale
    far = unit * (fine * lane * 128 % NLON)
    coarse = unit * (np.arange(KF // FINE, dtype=np.int64)[:, None] * FINE * lane % NLON)
    tables = [plus, minus, np.cos(far), np.sin(far), np.cos(coarse), np.sin(coarse)]
    return [np.asarray(t, dtype=np.float32) for t in tables]


def cell_requests(req_block, req_stencil, req_frac, counts):
    packed = (
        (req_block << 24)
        | (req_stencil[:, 0] << 20)
        | (req_stencil[:, 1] << 16)
        | (req_stencil[:, 2] << 12)
        | (req_stencil[:, 3] << 8)
        | (req_frac[:, 0] << 4)
        | req_frac[:, 1]
    )
    first = counts[0]
    second = first + counts[1]
    cells = jnp.zeros((COLS + CAP,), jnp.int32)
    cells = lax.dynamic_update_slice(cells, packed[0], (0,))
    cells = lax.dynamic_update_slice(cells, packed[1], (first,))
    cells = lax.dynamic_update_slice(cells, packed[2], (second,))
    return cells[:COLS].reshape(COLS // 128, 128), jnp.stack([first, second])


def decode(ends_ref, cells_ref, onehot_ref, weight_ref):
    rows = cells_ref.shape[0]
    columns = jnp.concatenate(
        [cells_ref[...], jnp.zeros((128 - rows, 128), jnp.int32)], axis=0
    ).T
    lane = lax.broadcasted_iota(jnp.int32, (128, 128), 1)
    sub = lax.broadcasted_iota(jnp.int32, (128, 128), 0)
    for row in range(rows):
        word = jnp.broadcast_to(columns[:, row : row + 1], (128, 128))
        block = lax.shift_right_logical(word, 24)
        edge = ends_ref[0] if row < rows // 2 else ends_ref[1]
        block = block + jnp.where(sub + row * 128 >= edge, BLOCKS, 0)
        here = pl.ds(row * 128, 128)
        for part in range(3):
            onehot_ref[here, part * 128 : (part + 1) * 128] = jnp.where(
                block == lane + part * 128, 1.0, 0.0
            ).astype(jnp.bfloat16)
        frac_lat = ((lax.shift_right_logical(word, 4) & 15).astype(jnp.float32) + 0.5) / FRAC
        frac_lon = ((word & 15).astype(jnp.float32) + 0.5) / FRAC
        corner = (
            (1.0 - frac_lat) * (1.0 - frac_lon),
            frac_lat * (1.0 - frac_lon),
            (1.0 - frac_lat) * frac_lon,
            frac_lat * frac_lon,
        )
        weight = jnp.zeros((128, 128), jnp.float32)
        for k in range(4):
            spot = lax.shift_right_logical(word, 20 - 4 * k) & 15
            weight = weight + jnp.where(spot == lane, corner[k], 0.0)
        weight_ref[here, :] = weight


def fill_table(small, plus, minus, table):
    near_plus, near_minus, far_cos, far_sin, coarse_cos, coarse_sin = small
    for sector in range(NLON // 128):
        here = pl.ds(sector * 128, 128)
        turn_cos = far_cos[:, sector : sector + 1]
        turn_sin = far_sin[:, sector : sector + 1]
        plus[:, here] = turn_cos * near_plus[...] + turn_sin * near_minus[...]
        minus[:, here] = turn_cos * near_minus[...] - turn_sin * near_plus[...]

    def body(step, carry):
        cos = coarse_cos[pl.ds(step, 1), :]
        sin = coarse_sin[pl.ds(step, 1), :]
        rows = pl.ds(pl.multiple_of(step * FINE, FINE), FINE)
        for sector in range(NLON // 128):
            here = slice(sector * 128, (sector + 1) * 128)
            table[sector // 2, rows, (sector % 2) * 128 : (sector % 2 + 1) * 128] = (
                cos * plus[:, here] + sin * minus[:, here]
            ).astype(jnp.bfloat16)
        return carry

    lax.fori_loop(0, KF // FINE, body, 0)


def ring_offset(step, count):
    return jnp.where(step % 2 == 1, (step + 1) // 2, count - step // 2)


def transform_kernel(
    lon,
    lat,
    ends_ref,
    cells_ref,
    left_ref,
    own_ref,
    right_ref,
    *refs,
):
    small, out_ref = refs[:6], refs[6]
    (tiles, onehot, weight, departed, sectors, plus, minus, table, total, blocks, landed, wide, packs, bands) = refs[7:21]
    send_row, recv_row, send_block, recv_block, send_band, recv_band = refs[21:]
    me_lon, me_lat = lax.axis_index("lon"), lax.axis_index("lat")
    rows = departed.shape[0]
    depth = blocks.shape[1]
    each = depth // lat
    chips = lon // 2

    barrier = pltpu.get_barrier_semaphore()

    def greet_lon(step, carry):
        peer = lax.rem(me_lon + step, lon)
        pl.semaphore_signal(barrier, inc=1, device_id={"lon": peer}, device_id_type=MESH)
        return carry

    def greet_lat(step, carry):
        peer = lax.rem(me_lat + step, lat)
        pl.semaphore_signal(barrier, inc=1, device_id={"lat": peer}, device_id_type=MESH)
        return carry

    lax.fori_loop(1, lon, greet_lon, 0)
    lax.fori_loop(1, lat, greet_lat, 0)

    tiles[:BLOCKS, :] = left_ref[...]
    tiles[BLOCKS : 2 * BLOCKS, :] = own_ref[...]
    tiles[2 * BLOCKS :, :] = right_ref[...]
    decode(ends_ref, cells_ref, onehot, weight)
    pl.semaphore_wait(barrier, lon + lat - 2)

    def row_copy(source, row, slot_send, slot_recv):
        return pltpu.make_async_remote_copy(
            src_ref=departed.at[row],
            dst_ref=sectors.at[source // 2, pl.ds(pl.multiple_of((source % 2) * 128, 128), 128), :],
            send_sem=send_row.at[slot_send],
            recv_sem=recv_row.at[slot_recv],
            device_id={"lon": row},
            device_id_type=MESH,
        )

    step = CHUNK * 128
    for part in range(rows // CHUNK):
        low = 0 if part * CHUNK < rows // 2 else BLOCKS
        here = pl.ds(part * step, step)
        values = jnp.zeros((step, 128), jnp.float32)
        for pair in range(BLK // 2):
            got = jnp.dot(
                onehot[here, :],
                tiles[low : low + 2 * BLOCKS, pair * 256 : (pair + 1) * 256],
                preferred_element_type=jnp.float32,
            )
            scale = weight[here, :]
            values = values + scale[:, 2 * pair : 2 * pair + 1] * got[:, :128]
            values = values + scale[:, 2 * pair + 1 : 2 * pair + 2] * got[:, 128:]
        departed[part * CHUNK : (part + 1) * CHUNK] = values.astype(jnp.bfloat16).reshape(CHUNK, 128, 128)

        def send_rows(row, carry):
            @pl.when(row != me_lon)
            def _():
                row_copy(me_lon, row, row, me_lon).start()

            return carry

        lax.fori_loop(part * CHUNK, (part + 1) * CHUNK, send_rows, 0)

    sectors[me_lon // 2, pl.ds(pl.multiple_of((me_lon % 2) * 128, 128), 128), :] = departed[me_lon]
    fill_table(small, plus, minus, table)
    total[...] = jnp.zeros_like(total)

    def gather_chip(chip):
        for core in range(2):
            source = chip * 2 + core

            @pl.when(source != me_lon)
            def _():
                row_copy(source, 0, source, source).wait_recv()

    def accumulate(step, carry):
        chip = lax.rem(me_lon // 2 + ring_offset(step, chips), chips)
        gather_chip(chip)
        for part in range(3):
            here = slice(part * (KF // 3), (part + 1) * (KF // 3))
            total[here, :] += jnp.dot(table[chip, here, :], sectors[chip], preferred_element_type=jnp.float32)
        return carry

    lax.fori_loop(0, chips, accumulate, 0)

    def block_copy(source, block, slot_send, slot_recv):
        return pltpu.make_async_remote_copy(
            src_ref=blocks.at[block],
            dst_ref=landed.at[source],
            send_sem=send_block.at[slot_send],
            recv_sem=recv_block.at[slot_recv],
            device_id={"lon": block},
            device_id_type=MESH,
        )

    blocks[...] = total[...].astype(jnp.bfloat16).reshape(blocks.shape)

    def send_blocks(step, carry):
        block = lax.rem(me_lon + step, lon)
        block_copy(me_lon, block, block, me_lon).start()
        return carry

    lax.fori_loop(1, lon, send_blocks, 0)
    wide[pl.ds(pl.multiple_of(me_lon * depth, depth), depth), :] = blocks[me_lon].astype(jnp.float32)

    def widen(step, carry):
        chip = lax.rem(me_lon // 2 + ring_offset(step, chips), chips)
        for core in range(2):
            source = chip * 2 + core

            @pl.when(source != me_lon)
            def _():
                block_copy(source, 0, source, source).wait_recv()
                wide[pl.ds(pl.multiple_of(source * depth, depth), depth), :] = landed[source].astype(jnp.float32)

        return carry

    lax.fori_loop(0, chips, widen, 0)

    def band_copy(source, target, slot_send, slot_recv):
        return pltpu.make_async_remote_copy(
            src_ref=packs.at[target],
            dst_ref=bands.at[source],
            send_sem=send_band.at[slot_send],
            recv_sem=recv_band.at[slot_recv],
            device_id={"lat": target},
            device_id_type=MESH,
        )

    def send_bands(step, carry):
        target = lax.rem(me_lat + step, lat)
        picked = [wide[pl.ds(target * each + k, lon, stride=depth), :] for k in range(each)]
        packs[target] = jnp.concatenate(picked, axis=0).astype(jnp.bfloat16)

        @pl.when(target != me_lat)
        def _():
            band_copy(me_lat, target, target, me_lat).start()

        return carry

    lax.fori_loop(1, lat + 1, send_bands, 0)
    bands[me_lat] = packs[me_lat]

    def finish_rows(step, carry):
        peer = lax.rem(me_lon + step, lon)
        row_copy(me_lon, peer, peer, me_lon).wait_send()
        block_copy(me_lon, peer, peer, me_lon).wait_send()
        return carry

    lax.fori_loop(1, lon, finish_rows, 0)

    def finish_bands(step, carry):
        peer = lax.rem(me_lat + step, lat)
        band_copy(peer, 0, peer, peer).wait_recv()
        band_copy(me_lat, peer, peer, me_lat).wait_send()
        return carry

    lax.fori_loop(1, lat, finish_bands, 0)
    out_ref[...] = bands[...]


def transform(lon, lat, ends, cells, left, own, right):
    vmem = pl.BlockSpec(memory_space=pltpu.VMEM)
    depth = KF // lon
    band = (lat, depth // lat * lon, 128)
    return pl.pallas_call(
        functools.partial(transform_kernel, lon, lat),
        out_shape=jax.ShapeDtypeStruct(band, jnp.bfloat16),
        in_specs=[pl.BlockSpec(memory_space=pltpu.SMEM)] + [vmem] * 10,
        out_specs=vmem,
        scratch_shapes=[
            pltpu.VMEM((3 * BLOCKS, BLK * 128), jnp.bfloat16),
            pltpu.VMEM((COLS, 2 * BLOCKS), jnp.bfloat16),
            pltpu.VMEM((COLS, 128), jnp.float32),
            pltpu.VMEM((COLS // 128, 128, 128), jnp.bfloat16),
            pltpu.VMEM((lon // 2, 256, 128), jnp.bfloat16),
            pltpu.VMEM((FINE, NLON), jnp.float32),
            pltpu.VMEM((FINE, NLON), jnp.float32),
            pltpu.VMEM((NLON // 256, KF, 256), jnp.bfloat16),
            pltpu.VMEM((KF, 128), jnp.float32),
            pltpu.VMEM((lon, depth, 128), jnp.bfloat16),
            pltpu.VMEM((lon, depth, 128), jnp.bfloat16),
            pltpu.VMEM((lon * depth, 128), jnp.float32),
            pltpu.VMEM(band, jnp.bfloat16),
            pltpu.VMEM(band, jnp.bfloat16),
            pltpu.SemaphoreType.DMA((lon,)),
            pltpu.SemaphoreType.DMA((lon,)),
            pltpu.SemaphoreType.DMA((lon,)),
            pltpu.SemaphoreType.DMA((lon,)),
            pltpu.SemaphoreType.DMA((lat,)),
            pltpu.SemaphoreType.DMA((lat,)),
        ],
        compiler_params=pltpu.CompilerParams(
            vmem_limit_bytes=48 << 20, collective_id=0, has_side_effects=True
        ),
        name="transform",
    )(ends, cells, left, own, right, *small_tables())


def gathered_bands(fields, req_block, req_stencil, req_frac, req_count):
    lon = lax.axis_size("lon")
    lat = lax.axis_size("lat")
    tile = fields.reshape(BLOCKS, BLK * 128)
    left = lax.ppermute(tile, "lon", [(i, (i + 1) % lon) for i in range(lon)])
    right = lax.ppermute(tile, "lon", [((i + 1) % lon, i) for i in range(lon)])
    cells, ends = cell_requests(req_block[0, 0], req_stencil[0, 0], req_frac[0, 0], req_count[0, 0])
    bands = transform(lon, lat, ends, cells, left, tile, right)
    own = KF // lon // lat
    bands = bands.reshape(lat, own, lon, 128).transpose(1, 0, 2, 3)
    return bands.reshape(own, lat * lon, 128)


def local(fields, req_block, req_stencil, req_frac, req_count, legendre):
    gathered = gathered_bands(fields, req_block, req_stencil, req_frac, req_count)
    projected = jnp.einsum("kyn,kyc->knc", legendre, gathered, preferred_element_type=jnp.float32)
    degree = jnp.arange(NN, dtype=jnp.float32)
    factor = 1.0 / (1.0 + 4.0 * degree * (degree + 1.0) / (NN * (NN + 1)))
    return projected * factor[None, :, None]


def solution(mesh):
    return jax.shard_map(
        local,
        mesh=mesh,
        in_specs=(
            P("lat", "lon", None),
            P("lat", "lon", None, None),
            P("lat", "lon", None, None, None),
            P("lat", "lon", None, None, None),
            P("lat", "lon", None),
            P(("lon", "lat"), None, None),
        ),
        out_specs=P(("lon", "lat"), None, None),
        check_vma=False,
    )
```

```python
import functools
import math

import jax
import jax.numpy as jnp
import numpy as np
from jax import lax
from jax.experimental import pallas as pl
from jax.experimental.pallas import tpu as pltpu
from jax.sharding import PartitionSpec as P

KF = 1536
NN = 768
BLK = 16
FRAC = 16
COLS = 3072
CAP = 1280
NLON = 3072
BLOCKS = COLS // BLK
FINE = 48
CHUNK = 4
MESH = pl.DeviceIdType.MESH


def small_tables():
    unit = 2.0 * math.pi / NLON
    fine = np.arange(FINE, dtype=np.int64)[:, None]
    lane = np.arange(128, dtype=np.int64)[None, :]
    scale = 1.0 / math.sqrt(NLON)
    near = unit * (fine * lane % NLON)
    plus = (np.cos(near) + np.sin(near)) * scale
    minus = (np.cos(near) - np.sin(near)) * scale
    far = unit * (fine * lane * 128 % NLON)
    coarse = unit * (np.arange(KF // FINE, dtype=np.int64)[:, None] * FINE * lane % NLON)
    tables = [plus, minus, np.cos(far), np.sin(far), np.cos(coarse), np.sin(coarse)]
    return np.concatenate(tables, axis=0).astype(np.float32)


def order_kernel(count_ref, block_ref, stencil_ref, frac_ref, cells_ref):
    first = count_ref[0]
    second = first + count_ref[1]
    lane = lax.broadcasted_iota(jnp.int32, (32, 128), 1)
    cell = lax.broadcasted_iota(jnp.int32, (32, 128), 0) * 128 + lane
    result = None
    for slot, start in ((0, None), (1, first), (2, second)):
        shift4 = 20 - 4 * lax.broadcasted_iota(jnp.int32, (4, CAP), 0)
        shift2 = 4 - 4 * lax.broadcasted_iota(jnp.int32, (2, CAP), 0)
        word = (
            lax.shift_left(block_ref[slot : slot + 1, :], jnp.full((1, CAP), 24, jnp.int32))
            + jnp.sum(lax.shift_left(stencil_ref[slot], shift4), axis=0, keepdims=True)
            + jnp.sum(lax.shift_left(frac_ref[slot], shift2), axis=0, keepdims=True)
        )
        pieces = [word[:, k * 128 : (k + 1) * 128] for k in range(CAP // 128)]
        pieces.append(jnp.zeros((32 - CAP // 128, 128), jnp.int32))
        placed = jnp.concatenate(pieces, axis=0)
        if start is None:
            result = placed
            continue
        turn = start % 128
        turned = pltpu.roll(placed, turn, 1)
        turned = jnp.where(lane < turn, pltpu.roll(turned, 1, 0), turned)
        result = jnp.where(cell < start, result, pltpu.roll(turned, start // 128, 0))
    cells_ref[...] = result[: cells_ref.shape[0], :]


def order_requests(count, block, stencil, frac):
    vmem = pl.BlockSpec(memory_space=pltpu.VMEM)
    return pl.pallas_call(
        order_kernel,
        out_shape=jax.ShapeDtypeStruct((COLS // 128, 128), jnp.int32),
        in_specs=[pl.BlockSpec(memory_space=pltpu.SMEM), vmem, vmem, vmem],
        out_specs=vmem,
        name="order_requests",
    )(count, block, stencil, frac)


def decode(first, second, cells_ref, onehot_ref, weight_ref):
    rows = cells_ref.shape[0]
    columns = jnp.concatenate(
        [cells_ref[...], jnp.zeros((128 - rows, 128), jnp.int32)], axis=0
    ).T
    lane = lax.broadcasted_iota(jnp.int32, (128, 128), 1)
    sub = lax.broadcasted_iota(jnp.int32, (128, 128), 0)
    for row in range(rows):
        word = jnp.broadcast_to(columns[:, row : row + 1], (128, 128))
        block = lax.shift_right_logical(word, 24)
        edge = first if row < rows // 2 else second
        block = block + jnp.where(sub + row * 128 >= edge, BLOCKS, 0)
        here = pl.ds(row * 128, 128)
        for part in range(3):
            onehot_ref[here, part * 128 : (part + 1) * 128] = jnp.where(
                block == lane + part * 128, 1.0, 0.0
            ).astype(jnp.bfloat16)
        frac_lat = ((lax.shift_right_logical(word, 4) & 15).astype(jnp.float32) + 0.5) / FRAC
        frac_lon = ((word & 15).astype(jnp.float32) + 0.5) / FRAC
        corner = (
            (1.0 - frac_lat) * (1.0 - frac_lon),
            frac_lat * (1.0 - frac_lon),
            (1.0 - frac_lat) * frac_lon,
            frac_lat * frac_lon,
        )
        weight = jnp.zeros((128, 128), jnp.float32)
        for k in range(4):
            spot = lax.shift_right_logical(word, 20 - 4 * k) & 15
            weight = weight + jnp.where(spot == lane, corner[k], 0.0)
        weight_ref[here, :] = weight


def fill_table(small, plus, minus, table):
    near_plus, near_minus, far_cos, far_sin = [small.at[pl.ds(k * FINE, FINE)] for k in range(4)]
    coarse_cos, coarse_sin = [small.at[pl.ds(4 * FINE + k * (KF // FINE), KF // FINE)] for k in range(2)]
    for sector in range(NLON // 128):
        here = pl.ds(sector * 128, 128)
        turn_cos = far_cos[:, sector : sector + 1]
        turn_sin = far_sin[:, sector : sector + 1]
        plus[:, here] = turn_cos * near_plus[...] + turn_sin * near_minus[...]
        minus[:, here] = turn_cos * near_minus[...] - turn_sin * near_plus[...]

    def body(step, carry):
        cos = coarse_cos[pl.ds(step, 1), :]
        sin = coarse_sin[pl.ds(step, 1), :]
        rows = pl.ds(pl.multiple_of(step * FINE, FINE), FINE)
        for sector in range(NLON // 128):
            here = slice(sector * 128, (sector + 1) * 128)
            table[sector // 2, rows, (sector % 2) * 128 : (sector % 2 + 1) * 128] = (
                cos * plus[:, here] + sin * minus[:, here]
            ).astype(jnp.bfloat16)
        return carry

    lax.fori_loop(0, KF // FINE, body, 0)


def near_first(step, count):
    return jnp.where(step % 2 == 1, (step + 1) // 2, count - step // 2)


def far_first(step, count):
    away = count // 2 - (step + 1) // 2
    return jnp.where(step % 2 == 1, away, count - away)


def transform_kernel(lon, lat, count_hbm, cells_hbm, own_hbm, table_ref, out_ref, *refs):
    (count_ref, cells_ref, own_ref, small, tiles, onehot, weight, departed, sectors, plus, minus, table, total, blocks, landed, wide, packs, bands) = refs[:18]
    fetch_sem, send_tile, recv_tile, send_row, recv_row, send_block, recv_block, send_band, recv_band = refs[18:]
    me_lon, me_lat = lax.axis_index("lon"), lax.axis_index("lat")
    rows = departed.shape[0]
    depth = blocks.shape[1]
    each = depth // lat
    chips = lon // 2
    me_chip = me_lon // 2
    tall = 8 if lat == 32 else lat
    flat = lat // tall

    barrier = pltpu.get_barrier_semaphore()

    def greet_lon(step, carry):
        peer = lax.rem(me_lon + step, lon)
        pl.semaphore_signal(barrier, inc=1, device_id={"lon": peer}, device_id_type=MESH)
        return carry

    def greet_lat(step, carry):
        peer = lax.rem(me_lat + step, lat)
        pl.semaphore_signal(barrier, inc=1, device_id={"lat": peer}, device_id_type=MESH)
        return carry

    lax.fori_loop(1, lon, greet_lon, 0)
    lax.fori_loop(1, lat, greet_lat, 0)
    pairs = ((own_hbm, own_ref), (count_hbm, count_ref), (cells_hbm, cells_ref), (table_ref, small))
    fetches = [pltpu.make_async_copy(src, dst, fetch_sem.at[k]) for k, (src, dst) in enumerate(pairs)]
    for fetch in fetches:
        fetch.start()
    fetches[0].wait()

    weight[...] = own_ref[...].astype(jnp.float32)
    for cell in range(BLK):
        tiles[BLOCKS : 2 * BLOCKS, cell * 128 : (cell + 1) * 128] = weight[
            pl.ds(cell, BLOCKS, stride=BLK), :
        ].astype(jnp.bfloat16)
    pl.semaphore_wait(barrier, lon + lat - 2)

    def tile_copy(side):
        return pltpu.make_async_remote_copy(
            src_ref=tiles.at[pl.ds(BLOCKS, BLOCKS)],
            dst_ref=tiles.at[pl.ds(2 * BLOCKS * side, BLOCKS)],
            send_sem=send_tile.at[side],
            recv_sem=recv_tile.at[side],
            device_id={"lon": lax.rem(me_lon + (1 if side == 0 else lon - 1), lon)},
            device_id_type=MESH,
        )

    for side in range(2):
        tile_copy(side).start()
    fetches[1].wait()
    fetches[2].wait()
    decode(count_ref[0], count_ref[0] + count_ref[1], cells_ref, onehot, weight)
    fetches[3].wait()
    fill_table(small, plus, minus, table)
    total[...] = jnp.zeros_like(total)
    for side in range(2):
        tile_copy(side).wait_recv()

    def row_copy(source, row, slot_send, slot_recv):
        return pltpu.make_async_remote_copy(
            src_ref=departed.at[row],
            dst_ref=sectors.at[source // 2, pl.ds(pl.multiple_of((source % 2) * 128, 128), 128), :],
            send_sem=send_row.at[slot_send],
            recv_sem=recv_row.at[slot_recv],
            device_id={"lon": row},
            device_id_type=MESH,
        )

    parts = rows // CHUNK

    def interpolate(turn, carry):
        part = lax.rem(me_lon // CHUNK + far_first(turn, parts), parts)
        low = pl.multiple_of(jnp.where(part < parts // 2, 0, BLOCKS), BLOCKS)
        here = pl.ds(pl.multiple_of(part * CHUNK * 128, CHUNK * 128), CHUNK * 128)
        values = jnp.zeros((CHUNK * 128, 128), jnp.float32)
        for pair in range(BLK // 2):
            got = jnp.dot(
                onehot[here, :],
                tiles[pl.ds(low, 2 * BLOCKS), pair * 256 : (pair + 1) * 256],
                preferred_element_type=jnp.float32,
            )
            scale = weight[here, :]
            values = values + scale[:, 2 * pair : 2 * pair + 1] * got[:, :128]
            values = values + scale[:, 2 * pair + 1 : 2 * pair + 2] * got[:, 128:]
        departed[pl.ds(part * CHUNK, CHUNK)] = values.astype(jnp.bfloat16).reshape(CHUNK, 128, 128)

        def send_rows(row, inner):
            @pl.when(row != me_lon)
            def _():
                row_copy(me_lon, row, row, me_lon).start()

            return inner

        lax.fori_loop(part * CHUNK, part * CHUNK + CHUNK, send_rows, 0)
        return carry

    lax.fori_loop(0, parts, interpolate, 0)
    sectors[me_chip, pl.ds(pl.multiple_of((me_lon % 2) * 128, 128), 128), :] = departed[me_lon]

    def accumulate(step, carry):
        chip = lax.rem(me_chip + near_first(step, chips), chips)
        for core in range(2):
            source = chip * 2 + core

            @pl.when(source != me_lon)
            def _():
                row_copy(source, 0, source, source).wait_recv()

        for part in range(3):
            here = slice(part * (KF // 3), (part + 1) * (KF // 3))
            total[here, :] += jnp.dot(table[chip, here, :], sectors[chip], preferred_element_type=jnp.float32)
        return carry

    lax.fori_loop(0, chips, accumulate, 0)

    def block_copy(source, block, slot_send, slot_recv):
        return pltpu.make_async_remote_copy(
            src_ref=blocks.at[block],
            dst_ref=landed.at[source],
            send_sem=send_block.at[slot_send],
            recv_sem=recv_block.at[slot_recv],
            device_id={"lon": block},
            device_id_type=MESH,
        )

    blocks[...] = total[...].astype(jnp.bfloat16).reshape(blocks.shape)

    def send_blocks(step, carry):
        chip = lax.rem(me_chip + far_first(step, chips), chips)
        for core in range(2):
            block = chip * 2 + core

            @pl.when(block != me_lon)
            def _():
                block_copy(me_lon, block, block, me_lon).start()

        return carry

    lax.fori_loop(0, chips, send_blocks, 0)
    wide[pl.ds(pl.multiple_of(me_lon * depth, depth), depth), :] = blocks[me_lon].astype(jnp.float32)

    def widen(step, carry):
        chip = lax.rem(me_chip + near_first(step, chips), chips)
        for core in range(2):
            source = chip * 2 + core

            @pl.when(source != me_lon)
            def _():
                block_copy(source, 0, source, source).wait_recv()
                wide[pl.ds(pl.multiple_of(source * depth, depth), depth), :] = landed[source].astype(jnp.float32)

        return carry

    lax.fori_loop(0, chips, widen, 0)

    def band_copy(source, target, slot_send, slot_recv):
        return pltpu.make_async_remote_copy(
            src_ref=packs.at[target],
            dst_ref=bands.at[source],
            send_sem=send_band.at[slot_send],
            recv_sem=recv_band.at[slot_recv],
            device_id={"lat": target},
            device_id_type=MESH,
        )

    def send_bands(step, carry):
        column = lax.rem(me_lat % flat + far_first(step // tall, flat), flat)
        target = lax.rem(me_lat // flat + far_first(step % tall, tall), tall) * flat + column
        picked = [wide[pl.ds(target * each + k, lon, stride=depth), :] for k in range(each)]
        packs[target] = jnp.concatenate(picked, axis=0).astype(jnp.bfloat16)

        @pl.when(target != me_lat)
        def _():
            band_copy(me_lat, target, target, me_lat).start()

        return carry

    lax.fori_loop(0, lat, send_bands, 0)
    bands[me_lat] = packs[me_lat]

    for side in range(2):
        tile_copy(side).wait_send()

    def finish_rows(step, carry):
        peer = lax.rem(me_lon + step, lon)
        row_copy(me_lon, peer, peer, me_lon).wait_send()
        block_copy(me_lon, peer, peer, me_lon).wait_send()
        return carry

    lax.fori_loop(1, lon, finish_rows, 0)

    def finish_bands(step, carry):
        peer = lax.rem(me_lat + step, lat)
        band_copy(peer, 0, peer, peer).wait_recv()
        band_copy(me_lat, peer, peer, me_lat).wait_send()
        return carry

    lax.fori_loop(1, lat, finish_bands, 0)
    out_ref[...] = bands[...]


def transform(lon, lat, count, cells, own):
    vmem = pl.BlockSpec(memory_space=pltpu.VMEM)
    depth = KF // lon
    band = (lat, depth // lat * lon, 128)
    small = small_tables()
    return pl.pallas_call(
        functools.partial(transform_kernel, lon, lat),
        out_shape=jax.ShapeDtypeStruct(band, jnp.bfloat16),
        in_specs=[pl.BlockSpec(memory_space=pltpu.HBM)] * 4,
        out_specs=vmem,
        scratch_shapes=[
            pltpu.SMEM((3,), jnp.int32),
            pltpu.VMEM((COLS // 128, 128), jnp.int32),
            pltpu.VMEM((COLS, 128), jnp.bfloat16),
            pltpu.VMEM(small.shape, jnp.float32),
            pltpu.VMEM((3 * BLOCKS, BLK * 128), jnp.bfloat16),
            pltpu.VMEM((COLS, 2 * BLOCKS), jnp.bfloat16),
            pltpu.VMEM((COLS, 128), jnp.float32),
            pltpu.VMEM((COLS // 128, 128, 128), jnp.bfloat16),
            pltpu.VMEM((lon // 2, 256, 128), jnp.bfloat16),
            pltpu.VMEM((FINE, NLON), jnp.float32),
            pltpu.VMEM((FINE, NLON), jnp.float32),
            pltpu.VMEM((NLON // 256, KF, 256), jnp.bfloat16),
            pltpu.VMEM((KF, 128), jnp.float32),
            pltpu.VMEM((lon, depth, 128), jnp.bfloat16),
            pltpu.VMEM((lon, depth, 128), jnp.bfloat16),
            pltpu.VMEM((lon * depth, 128), jnp.float32),
            pltpu.VMEM(band, jnp.bfloat16),
            pltpu.VMEM(band, jnp.bfloat16),
            pltpu.SemaphoreType.DMA((4,)),
            pltpu.SemaphoreType.DMA((2,)),
            pltpu.SemaphoreType.DMA((2,)),
            pltpu.SemaphoreType.DMA((lon,)),
            pltpu.SemaphoreType.DMA((lon,)),
            pltpu.SemaphoreType.DMA((lon,)),
            pltpu.SemaphoreType.DMA((lon,)),
            pltpu.SemaphoreType.DMA((lat,)),
            pltpu.SemaphoreType.DMA((lat,)),
        ],
        compiler_params=pltpu.CompilerParams(
            vmem_limit_bytes=62976 << 10, collective_id=0, has_side_effects=True
        ),
        name="transform",
    )(count, cells, own, small)


def gathered_bands(fields, req_block, req_stencil, req_frac, req_count):
    lon = lax.axis_size("lon")
    lat = lax.axis_size("lat")
    count = req_count[0, 0]
    cells = order_requests(count, req_block[0, 0], req_stencil[0, 0], req_frac[0, 0])
    bands = transform(lon, lat, count, cells, fields.reshape(COLS, 128))
    own = KF // lon // lat
    bands = bands.reshape(lat, own, lon, 128).transpose(1, 0, 2, 3)
    return bands.reshape(own, lat * lon, 128)


def local(fields, req_block, req_stencil, req_frac, req_count, legendre):
    gathered = gathered_bands(fields, req_block, req_stencil, req_frac, req_count)
    projected = jnp.einsum("kyn,kyc->knc", legendre, gathered, preferred_element_type=jnp.float32)
    degree = jnp.arange(NN, dtype=jnp.float32)
    factor = 1.0 / (1.0 + 4.0 * degree * (degree + 1.0) / (NN * (NN + 1)))
    return projected * factor[None, :, None]


def solution(mesh):
    return jax.shard_map(
        local,
        mesh=mesh,
        in_specs=(
            P("lat", "lon", None),
            P("lat", "lon", None, None),
            P("lat", "lon", None, None, None),
            P("lat", "lon", None, None, None),
            P("lat", "lon", None),
            P(("lon", "lat"), None, None),
        ),
        out_specs=P(("lon", "lat"), None, None),
        check_vma=False,
    )
```

```python
import functools
import math

import jax
import jax.numpy as jnp
import numpy as np
from jax import lax
from jax.experimental import pallas as pl
from jax.experimental.pallas import tpu as pltpu
from jax.sharding import PartitionSpec as P

KF = 1536
NN = 768
BLK = 16
FRAC = 16
COLS = 3072
CAP = 1280
NLON = 3072
BLOCKS = COLS // BLK
FINE = 96
CHUNK = 4
MESH = pl.DeviceIdType.MESH


def small_tables():
    unit = 2.0 * math.pi / NLON
    fine = np.concatenate([np.arange(0, FINE, 2), np.arange(1, FINE, 2)]).astype(np.int64)[:, None]
    lane = np.arange(128, dtype=np.int64)[None, :]
    scale = 1.0 / math.sqrt(NLON)
    near = unit * (fine * lane % NLON)
    plus = (np.cos(near) + np.sin(near)) * scale
    minus = (np.cos(near) - np.sin(near)) * scale
    far = unit * (fine * lane * 128 % NLON)
    coarse = unit * (np.arange(KF // FINE, dtype=np.int64)[:, None] * FINE * lane % NLON)
    tables = [plus, minus, np.cos(far), np.sin(far), np.cos(coarse), np.sin(coarse)]
    return np.concatenate(tables, axis=0).astype(np.float32)


def order_requests(first, second, block_ref, stencil_ref, frac_ref, cells_ref):
    lane = lax.broadcasted_iota(jnp.int32, (32, 128), 1)
    cell = lax.broadcasted_iota(jnp.int32, (32, 128), 0) * 128 + lane
    shift4 = 20 - 4 * lax.broadcasted_iota(jnp.int32, (4, CAP), 0)
    shift2 = 4 - 4 * lax.broadcasted_iota(jnp.int32, (2, CAP), 0)
    result = None
    for slot, start in ((0, None), (1, first), (2, second)):
        word = (
            lax.shift_left(block_ref[slot], jnp.full((1, CAP), 24, jnp.int32))
            + jnp.sum(lax.shift_left(stencil_ref[slot], shift4), axis=0, keepdims=True)
            + jnp.sum(lax.shift_left(frac_ref[slot], shift2), axis=0, keepdims=True)
        )
        pieces = [word[:, k * 128 : (k + 1) * 128] for k in range(CAP // 128)]
        pieces.append(jnp.zeros((32 - CAP // 128, 128), jnp.int32))
        placed = jnp.concatenate(pieces, axis=0)
        if start is None:
            result = placed
            continue
        moved = jnp.full((32, 128), start, jnp.int32)
        for bit in range(12):
            if bit < 7:
                turned = pltpu.roll(placed, 1 << bit, 1)
                turned = jnp.where(lane < (1 << bit), pltpu.roll(turned, 1, 0), turned)
            else:
                turned = pltpu.roll(placed, 1 << (bit - 7), 0)
            chosen = lax.shift_right_logical(moved, jnp.full((32, 128), bit, jnp.int32)) & 1
            placed = jnp.where(chosen == 1, turned, placed)
        result = jnp.where(cell < moved, result, placed)
    cells_ref[...] = result[: cells_ref.shape[0], :]


def decode(first, second, cells_ref, onehot_ref, weight_ref):
    rows = cells_ref.shape[0]
    columns = jnp.concatenate(
        [cells_ref[...], jnp.zeros((128 - rows, 128), jnp.int32)], axis=0
    ).T
    lane = lax.broadcasted_iota(jnp.int32, (128, 128), 1)
    sub = lax.broadcasted_iota(jnp.int32, (128, 128), 0)
    for row in range(rows):
        word = jnp.broadcast_to(columns[:, row : row + 1], (128, 128))
        block = lax.shift_right_logical(word, 24)
        edge = first if row < rows // 2 else second
        block = block + jnp.where(sub + row * 128 >= edge, BLOCKS, 0)
        here = pl.ds(row * 128, 128)
        for part in range(3):
            onehot_ref[here, part * 128 : (part + 1) * 128] = jnp.where(
                block == lane + part * 128, 1.0, 0.0
            ).astype(jnp.bfloat16)
        frac_lat = ((lax.shift_right_logical(word, 4) & 15).astype(jnp.float32) + 0.5) / FRAC
        frac_lon = ((word & 15).astype(jnp.float32) + 0.5) / FRAC
        corner = (
            (1.0 - frac_lat) * (1.0 - frac_lon),
            frac_lat * (1.0 - frac_lon),
            (1.0 - frac_lat) * frac_lon,
            frac_lat * frac_lon,
        )
        weight = jnp.zeros((128, 128), jnp.float32)
        for k in range(4):
            spot = lax.shift_right_logical(word, 20 - 4 * k) & 15
            weight = weight + jnp.where(spot == lane, corner[k], 0.0)
        weight_ref[here, :] = weight


def fill_table(small, plus, minus, table):
    near_plus, near_minus, far_cos, far_sin = [small.at[pl.ds(k * FINE, FINE)] for k in range(4)]
    coarse_cos, coarse_sin = [small.at[pl.ds(4 * FINE + k * (KF // FINE), KF // FINE)] for k in range(2)]
    for sector in range(NLON // 128):
        here = pl.ds(sector * 128, 128)
        turn_cos = far_cos[:, sector : sector + 1]
        turn_sin = far_sin[:, sector : sector + 1]
        plus[:, here] = turn_cos * near_plus[...] + turn_sin * near_minus[...]
        minus[:, here] = turn_cos * near_minus[...] - turn_sin * near_plus[...]

    def body(step, carry):
        cos = coarse_cos[pl.ds(step, 1), :]
        sin = coarse_sin[pl.ds(step, 1), :]
        for parity in range(2):
            here = slice(parity * (FINE // 2), (parity + 1) * (FINE // 2))
            rows = pl.ds(pl.multiple_of(step * (FINE // 2), FINE // 2) + parity * (KF // 2), FINE // 2)
            for sector in range(NLON // 128):
                lanes = slice(sector * 128, (sector + 1) * 128)
                table[sector // 2, rows, (sector % 2) * 128 : (sector % 2 + 1) * 128] = (
                    cos * plus[here, lanes] + sin * minus[here, lanes]
                ).astype(jnp.bfloat16)
        return carry

    lax.fori_loop(0, KF // FINE, body, 0)


def near_first(step, count):
    return jnp.where(step % 2 == 1, (step + 1) // 2, count - step // 2)


def far_first(step, count):
    away = count // 2 - (step + 1) // 2
    return jnp.where(step % 2 == 1, away, count - away)


def transform_kernel(lon, lat, count_hbm, block_hbm, stencil_hbm, frac_hbm, own_hbm, table_hbm, out_ref, *refs):
    (count_ref, block_ref, stencil_ref, frac_ref, own_ref, small) = refs[:6]
    (cells_ref, tiles, onehot, weight, departed, sectors, detour, plus, minus, table, total) = refs[6:17]
    (blocks, landed, bypass, wide, packs, bands) = refs[17:23]
    (fetch_sem, send_tile, recv_tile, send_row, recv_row, detour_sem, onward_row) = refs[23:30]
    (send_block, recv_block, bypass_sem, onward_block, send_band, recv_band) = refs[30:]
    me_lon, me_lat = lax.axis_index("lon"), lax.axis_index("lat")
    rows = departed.shape[0]
    depth = blocks.shape[2]
    each = depth // lat
    chips = lon // 2
    me_chip, me_core = me_lon // 2, me_lon % 2
    tall = 8 if lat == 32 else lat
    flat = lat // tall
    quarter = (chips // 4, chips - chips // 4)

    barrier = pltpu.get_barrier_semaphore()

    def greet_lon(step, carry):
        peer = lax.rem(me_lon + step, lon)
        pl.semaphore_signal(barrier, inc=1, device_id={"lon": peer}, device_id_type=MESH)
        return carry

    def greet_lat(step, carry):
        peer = lax.rem(me_lat + step, lat)
        pl.semaphore_signal(barrier, inc=1, device_id={"lat": peer}, device_id_type=MESH)
        return carry

    lax.fori_loop(1, lon, greet_lon, 0)
    lax.fori_loop(1, lat, greet_lat, 0)
    pairs = (
        (own_hbm, own_ref),
        (count_hbm, count_ref),
        (block_hbm, block_ref),
        (stencil_hbm, stencil_ref),
        (frac_hbm, frac_ref),
        (table_hbm, small),
    )
    fetches = [pltpu.make_async_copy(src, dst, fetch_sem.at[k]) for k, (src, dst) in enumerate(pairs)]
    for fetch in fetches:
        fetch.start()
    fetches[0].wait()

    weight[...] = own_ref[...].astype(jnp.float32)
    for cell in range(BLK):
        tiles[BLOCKS : 2 * BLOCKS, cell * 128 : (cell + 1) * 128] = weight[
            pl.ds(cell, BLOCKS, stride=BLK), :
        ].astype(jnp.bfloat16)
    pl.semaphore_wait(barrier, lon + lat - 2)

    def tile_copy(side):
        return pltpu.make_async_remote_copy(
            src_ref=tiles.at[pl.ds(BLOCKS, BLOCKS)],
            dst_ref=tiles.at[pl.ds(2 * BLOCKS * side, BLOCKS)],
            send_sem=send_tile.at[side],
            recv_sem=recv_tile.at[side],
            device_id={"lon": lax.rem(me_lon + jnp.where(side == 0, 1, lon - 1), lon)},
            device_id_type=MESH,
        )

    tile_copy(me_core).start()
    tile_copy(1 - me_core).start()
    for fetch in fetches[1:]:
        fetch.wait()
    first = count_ref[0]
    second = first + count_ref[1]
    order_requests(first, second, block_ref, stencil_ref, frac_ref, cells_ref)
    decode(first, second, cells_ref, onehot, weight)

    def slot_of(source):
        return sectors.at[source // 2, pl.ds(pl.multiple_of((source % 2) * 128, 128), 128), :]

    def row_copy(source, row, slot_send, slot_recv):
        return pltpu.make_async_remote_copy(
            src_ref=departed.at[row],
            dst_ref=slot_of(source),
            send_sem=send_row.at[slot_send],
            recv_sem=recv_row.at[slot_recv],
            device_id={"lon": row},
            device_id_type=MESH,
        )

    def row_detour(row, core):
        return pltpu.make_async_remote_copy(
            src_ref=departed.at[row],
            dst_ref=detour.at[core],
            send_sem=send_row.at[row],
            recv_sem=detour_sem.at[core],
            device_id={"lon": lax.rem(me_chip + quarter[core], chips) * 2 + me_core},
            device_id_type=MESH,
        )

    def row_onward(core):
        source = lax.rem(me_chip + chips - quarter[core], chips) * 2 + me_core
        return pltpu.make_async_remote_copy(
            src_ref=detour.at[core],
            dst_ref=slot_of(source),
            send_sem=onward_row.at[core],
            recv_sem=recv_row.at[source],
            device_id={"lon": lax.rem(me_chip + quarter[core], chips) * 2 + core},
            device_id_type=MESH,
        )

    parts = rows // CHUNK

    def interpolate(part, carry):
        low = pl.multiple_of(jnp.where(part < parts // 2, 0, BLOCKS), BLOCKS)
        here = pl.ds(pl.multiple_of(part * CHUNK * 128, CHUNK * 128), CHUNK * 128)
        values = jnp.zeros((CHUNK * 128, 128), jnp.float32)
        for pair in range(BLK // 2):
            got = jnp.dot(
                onehot[here, :],
                tiles[pl.ds(low, 2 * BLOCKS), pair * 256 : (pair + 1) * 256],
                preferred_element_type=jnp.float32,
            )
            scale = weight[here, :]
            values = values + scale[:, 2 * pair : 2 * pair + 1] * got[:, :128]
            values = values + scale[:, 2 * pair + 1 : 2 * pair + 2] * got[:, 128:]
        departed[pl.ds(part * CHUNK, CHUNK)] = values.astype(jnp.bfloat16).reshape(CHUNK, 128, 128)

        def send_rows(pair, inner):
            chip = part * (CHUNK // 2) + pair
            opposite = lax.rem(chip + chips - me_chip, chips) == chips // 2
            for core in range(2):
                row = chip * 2 + core

                @pl.when(opposite)
                def _():
                    row_detour(row, core).start()

                @pl.when(jnp.logical_and(jnp.logical_not(opposite), row != me_lon))
                def _():
                    row_copy(me_lon, row, row, me_lon).start()

            return inner

        lax.fori_loop(0, CHUNK // 2, send_rows, 0)
        return carry

    for turn in range(2):
        half = 1 - me_core if turn == 0 else me_core
        tile_copy(half).wait_recv()
        lax.fori_loop(half * (parts // 2), (half + 1) * (parts // 2), interpolate, 0)
    slot_of(me_lon)[...] = departed[me_lon]
    fill_table(small, plus, minus, table)
    total[...] = jnp.zeros_like(total)
    for core in range(2):
        row_detour(0, core).wait_recv()
        row_onward(core).start()

    def accumulate(step, carry):
        chip = lax.rem(me_chip + near_first(step, chips), chips)
        for core in range(2):
            source = chip * 2 + core

            @pl.when(source != me_lon)
            def _():
                row_copy(source, 0, source, source).wait_recv()

        for part in range(3):
            here = slice(part * (KF // 3), (part + 1) * (KF // 3))
            total[here, :] += jnp.dot(table[chip, here, :], sectors[chip], preferred_element_type=jnp.float32)
        return carry

    lax.fori_loop(0, chips, accumulate, 0)

    def block_copy(parity, source, block, slot_send, slot_recv):
        return pltpu.make_async_remote_copy(
            src_ref=blocks.at[parity, block],
            dst_ref=landed.at[parity, source],
            send_sem=send_block.at[parity, slot_send],
            recv_sem=recv_block.at[parity, slot_recv],
            device_id={"lon": block},
            device_id_type=MESH,
        )

    def block_detour(parity, core):
        block = lax.rem(me_chip + chips // 2, chips) * 2 + core
        return pltpu.make_async_remote_copy(
            src_ref=blocks.at[parity, block],
            dst_ref=bypass.at[parity, core],
            send_sem=send_block.at[parity, block],
            recv_sem=bypass_sem.at[parity, core],
            device_id={"lon": lax.rem(me_chip + quarter[core], chips) * 2 + me_core},
            device_id_type=MESH,
        )

    def block_onward(parity, core):
        source = lax.rem(me_chip + chips - quarter[core], chips) * 2 + me_core
        return pltpu.make_async_remote_copy(
            src_ref=bypass.at[parity, core],
            dst_ref=landed.at[parity, source],
            send_sem=onward_block.at[parity, core],
            recv_sem=recv_block.at[parity, source],
            device_id={"lon": lax.rem(me_chip + quarter[core], chips) * 2 + core},
            device_id_type=MESH,
        )

    blocks[...] = total[...].astype(jnp.bfloat16).reshape(blocks.shape)
    for parity in range(2):
        for core in range(2):
            block_detour(parity, core).start()
    for parity in range(2):

        def send_blocks(step, carry):
            chip = lax.rem(me_chip + far_first(step, chips), chips)
            for core in range(2):
                block = chip * 2 + core

                @pl.when(block != me_lon)
                def _():
                    block_copy(parity, me_lon, block, block, me_lon).start()

            return carry

        lax.fori_loop(1, chips, send_blocks, 0)
    for parity in range(2):
        for core in range(2):
            block_detour(parity, core).wait_recv()
            block_onward(parity, core).start()

    def band_copy(parity, source, target, slot_send, slot_recv):
        return pltpu.make_async_remote_copy(
            src_ref=packs.at[parity, target],
            dst_ref=bands.at[parity, source],
            send_sem=send_band.at[parity, slot_send],
            recv_sem=recv_band.at[parity, slot_recv],
            device_id={"lat": target},
            device_id_type=MESH,
        )

    for parity in range(2):
        wide[parity, pl.ds(pl.multiple_of(me_lon * depth, depth), depth), :] = blocks[parity, me_lon].astype(jnp.float32)

        def widen(step, carry):
            chip = lax.rem(me_chip + near_first(step, chips), chips)
            for core in range(2):
                source = chip * 2 + core

                @pl.when(source != me_lon)
                def _():
                    block_copy(parity, source, 0, source, source).wait_recv()
                    here = pl.ds(pl.multiple_of(source * depth, depth), depth)
                    wide[parity, here, :] = landed[parity, source].astype(jnp.float32)

            return carry

        lax.fori_loop(0, chips, widen, 0)

        def send_bands(step, carry):
            column = lax.rem(me_lat % flat + far_first(step // tall, flat), flat)
            target = lax.rem(me_lat // flat + far_first(step % tall, tall), tall) * flat + column
            picked = [wide[parity, pl.ds(target * each + k, lon, stride=depth), :] for k in range(each)]
            packs[parity, target] = jnp.concatenate(picked, axis=0).astype(jnp.bfloat16)

            @pl.when(target != me_lat)
            def _():
                band_copy(parity, me_lat, target, target, me_lat).start()

            return carry

        lax.fori_loop(0, lat, send_bands, 0)
        bands[parity, me_lat] = packs[parity, me_lat]

    for side in range(2):
        tile_copy(side).wait_send()
        row_onward(side).wait_send()

    def finish_rows(step, carry):
        peer = lax.rem(me_lon + step, lon)
        row_copy(me_lon, peer, peer, me_lon).wait_send()
        for parity in range(2):
            block_copy(parity, me_lon, peer, peer, me_lon).wait_send()
        return carry

    lax.fori_loop(1, lon, finish_rows, 0)
    for parity in range(2):
        for core in range(2):
            block_onward(parity, core).wait_send()

    def finish_bands(step, carry):
        peer = lax.rem(me_lat + step, lat)
        for parity in range(2):
            band_copy(parity, peer, 0, peer, peer).wait_recv()
            band_copy(parity, me_lat, peer, peer, me_lat).wait_send()
        return carry

    lax.fori_loop(1, lat, finish_bands, 0)
    out_ref[...] = bands[...]


def transform(lon, lat, count, block, stencil, frac, own):
    depth = KF // lon // 2
    band = (2, lat, depth // lat * lon, 128)
    small = small_tables()
    return pl.pallas_call(
        functools.partial(transform_kernel, lon, lat),
        out_shape=jax.ShapeDtypeStruct(band, jnp.bfloat16),
        in_specs=[pl.BlockSpec(memory_space=pltpu.HBM)] * 6,
        out_specs=pl.BlockSpec(memory_space=pltpu.VMEM),
        scratch_shapes=[
            pltpu.SMEM((3,), jnp.int32),
            pltpu.VMEM(block.shape, jnp.int32),
            pltpu.VMEM(stencil.shape, jnp.int32),
            pltpu.VMEM(frac.shape, jnp.int32),
            pltpu.VMEM((COLS, 128), jnp.bfloat16),
            pltpu.VMEM(small.shape, jnp.float32),
            pltpu.VMEM((COLS // 128, 128), jnp.int32),
            pltpu.VMEM((3 * BLOCKS, BLK * 128), jnp.bfloat16),
            pltpu.VMEM((COLS, 2 * BLOCKS), jnp.bfloat16),
            pltpu.VMEM((COLS, 128), jnp.float32),
            pltpu.VMEM((COLS // 128, 128, 128), jnp.bfloat16),
            pltpu.VMEM((lon // 2, 256, 128), jnp.bfloat16),
            pltpu.VMEM((2, 128, 128), jnp.bfloat16),
            pltpu.VMEM((FINE, NLON), jnp.float32),
            pltpu.VMEM((FINE, NLON), jnp.float32),
            pltpu.VMEM((NLON // 256, KF, 256), jnp.bfloat16),
            pltpu.VMEM((KF, 128), jnp.float32),
            pltpu.VMEM((2, lon, depth, 128), jnp.bfloat16),
            pltpu.VMEM((2, lon, depth, 128), jnp.bfloat16),
            pltpu.VMEM((2, 2, depth, 128), jnp.bfloat16),
            pltpu.VMEM((2, lon * depth, 128), jnp.float32),
            pltpu.VMEM(band, jnp.bfloat16),
            pltpu.VMEM(band, jnp.bfloat16),
            pltpu.SemaphoreType.DMA((6,)),
            pltpu.SemaphoreType.DMA((2,)),
            pltpu.SemaphoreType.DMA((2,)),
            pltpu.SemaphoreType.DMA((lon,)),
            pltpu.SemaphoreType.DMA((lon,)),
            pltpu.SemaphoreType.DMA((2,)),
            pltpu.SemaphoreType.DMA((2,)),
            pltpu.SemaphoreType.DMA((2, lon)),
            pltpu.SemaphoreType.DMA((2, lon)),
            pltpu.SemaphoreType.DMA((2, 2)),
            pltpu.SemaphoreType.DMA((2, 2)),
            pltpu.SemaphoreType.DMA((2, lat)),
            pltpu.SemaphoreType.DMA((2, lat)),
        ],
        compiler_params=pltpu.CompilerParams(
            vmem_limit_bytes=62976 << 10, collective_id=0, has_side_effects=True
        ),
        name="transform",
    )(count, block, stencil, frac, own, small)


def gathered_bands(fields, req_block, req_stencil, req_frac, req_count):
    lon = lax.axis_size("lon")
    lat = lax.axis_size("lat")
    block = req_block[0, 0].reshape(3, 1, CAP)
    bands = transform(
        lon, lat, req_count[0, 0], block, req_stencil[0, 0], req_frac[0, 0], fields.reshape(COLS, 128)
    )
    half = KF // lon // lat // 2
    bands = bands.reshape(2, lat, half, lon, 128).transpose(2, 0, 1, 3, 4)
    return bands.reshape(2 * half, lat * lon, 128)


def local(fields, req_block, req_stencil, req_frac, req_count, legendre):
    gathered = gathered_bands(fields, req_block, req_stencil, req_frac, req_count)
    projected = jnp.einsum("kyn,kyc->knc", legendre, gathered, preferred_element_type=jnp.float32)
    degree = jnp.arange(NN, dtype=jnp.float32)
    factor = 1.0 / (1.0 + 4.0 * degree * (degree + 1.0) / (NN * (NN + 1)))
    return projected * factor[None, :, None]


def solution(mesh):
    return jax.shard_map(
        local,
        mesh=mesh,
        in_specs=(
            P("lat", "lon", None),
            P("lat", "lon", None, None),
            P("lat", "lon", None, None, None),
            P("lat", "lon", None, None, None),
            P("lat", "lon", None),
            P(("lon", "lat"), None, None),
        ),
        out_specs=P(("lon", "lat"), None, None),
        check_vma=False,
    )
```

```python
import functools
import math

import jax
import jax.numpy as jnp
import numpy as np
from jax import lax
from jax.experimental import pallas as pl
from jax.experimental.pallas import tpu as pltpu
from jax.sharding import PartitionSpec as P

KF = 1536
NN = 768
BLK = 16
FRAC = 16
COLS = 3072
CAP = 1280
NLON = 3072
BLOCKS = COLS // BLK
FINE = 96
CHUNK = 4
EDGE = CAP // 128
MESH = pl.DeviceIdType.MESH


def small_tables():
    unit = 2.0 * math.pi / NLON
    fine = np.concatenate([np.arange(0, FINE, 2), np.arange(1, FINE, 2)]).astype(np.int64)[:, None]
    lane = np.arange(128, dtype=np.int64)[None, :]
    scale = 1.0 / math.sqrt(NLON)
    near = unit * (fine * lane % NLON)
    plus = (np.cos(near) + np.sin(near)) * scale
    minus = (np.cos(near) - np.sin(near)) * scale
    far = unit * (fine * lane * 128 % NLON)
    coarse = unit * (np.arange(KF // FINE, dtype=np.int64)[:, None] * FINE * lane % NLON)
    tables = [plus, minus, np.cos(far), np.sin(far), np.cos(coarse), np.sin(coarse)]
    return np.concatenate(tables, axis=0).astype(np.float32)


def order_requests(first, second, block_ref, stencil_ref, frac_ref, outbox, cells_ref):
    lane = lax.broadcasted_iota(jnp.int32, (32, 128), 1)
    cell = lax.broadcasted_iota(jnp.int32, (32, 128), 0) * 128 + lane
    shift4 = 20 - 4 * lax.broadcasted_iota(jnp.int32, (4, CAP), 0)
    shift2 = 4 - 4 * lax.broadcasted_iota(jnp.int32, (2, CAP), 0)
    result = None
    for slot, start in ((0, None), (1, first), (2, second)):
        word = (
            lax.shift_left(block_ref[slot], jnp.full((1, CAP), 24, jnp.int32))
            + jnp.sum(lax.shift_left(stencil_ref[slot], shift4), axis=0, keepdims=True)
            + jnp.sum(lax.shift_left(frac_ref[slot], shift2), axis=0, keepdims=True)
        )
        pieces = [word[:, k * 128 : (k + 1) * 128] for k in range(CAP // 128)]
        pieces.append(jnp.zeros((32 - CAP // 128, 128), jnp.int32))
        placed = jnp.concatenate(pieces, axis=0)
        if start is None:
            result = placed
            continue
        moved = jnp.full((32, 128), start, jnp.int32)
        for bit in range(12):
            if bit < 7:
                turned = pltpu.roll(placed, 1 << bit, 1)
                turned = jnp.where(lane < (1 << bit), pltpu.roll(turned, 1, 0), turned)
            else:
                turned = pltpu.roll(placed, 1 << (bit - 7), 0)
            chosen = lax.shift_right_logical(moved, jnp.full((32, 128), bit, jnp.int32)) & 1
            placed = jnp.where(chosen == 1, turned, placed)
        result = jnp.where(cell < moved, result, placed)
    rows = cells_ref.shape[0]
    nobody = -(1 << 24)
    outbox[0] = jnp.where(cell < first, result, result | nobody)[:rows, :]
    late = jnp.where(cell >= second, result, result | nobody)
    outbox[1] = pltpu.roll(late, 32 - rows + EDGE, 0)[:rows, :]
    middle = jnp.where(jnp.logical_and(cell >= first, cell < second), result, result | nobody)
    cells_ref[...] = middle[:rows, :]


def decode(words, chosen, base, onehot_ref, weight_ref):
    columns = jnp.concatenate(
        [words, jnp.zeros((128 - words.shape[0], 128), jnp.int32)], axis=0
    ).T
    lane = lax.broadcasted_iota(jnp.int32, (128, 128), 1)
    for place, row in enumerate(chosen):
        word = jnp.broadcast_to(columns[:, row : row + 1], (128, 128))
        block = lax.shift_right_logical(word, 24)
        here = pl.ds(pl.multiple_of(base + place * 128, 128), 128)
        for part in range(2):
            onehot_ref[here, part * 128 : (part + 1) * 128] = jnp.where(
                block == lane + part * 128, 1.0, 0.0
            ).astype(jnp.bfloat16)
        frac_lat = ((lax.shift_right_logical(word, 4) & 15).astype(jnp.float32) + 0.5) / FRAC
        frac_lon = ((word & 15).astype(jnp.float32) + 0.5) / FRAC
        corner = (
            (1.0 - frac_lat) * (1.0 - frac_lon),
            frac_lat * (1.0 - frac_lon),
            (1.0 - frac_lat) * frac_lon,
            frac_lat * frac_lon,
        )
        weight = jnp.zeros((128, 128), jnp.float32)
        for k in range(4):
            spot = lax.shift_right_logical(word, 20 - 4 * k) & 15
            weight = weight + jnp.where(spot == lane, corner[k], 0.0)
        weight_ref[here, :] = weight


def fill_table(small, plus, minus, table):
    near_plus, near_minus, far_cos, far_sin = [small.at[pl.ds(k * FINE, FINE)] for k in range(4)]
    coarse_cos, coarse_sin = [small.at[pl.ds(4 * FINE + k * (KF // FINE), KF // FINE)] for k in range(2)]
    for sector in range(NLON // 128):
        here = pl.ds(sector * 128, 128)
        turn_cos = far_cos[:, sector : sector + 1]
        turn_sin = far_sin[:, sector : sector + 1]
        plus[:, here] = turn_cos * near_plus[...] + turn_sin * near_minus[...]
        minus[:, here] = turn_cos * near_minus[...] - turn_sin * near_plus[...]

    def body(step, carry):
        cos = coarse_cos[pl.ds(step, 1), :]
        sin = coarse_sin[pl.ds(step, 1), :]
        for parity in range(2):
            here = slice(parity * (FINE // 2), (parity + 1) * (FINE // 2))
            rows = pl.ds(pl.multiple_of(step * (FINE // 2), FINE // 2) + parity * (KF // 2), FINE // 2)
            for sector in range(NLON // 128):
                lanes = slice(sector * 128, (sector + 1) * 128)
                table[sector // 2, rows, (sector % 2) * 128 : (sector % 2 + 1) * 128] = (
                    cos * plus[here, lanes] + sin * minus[here, lanes]
                ).astype(jnp.bfloat16)
        return carry

    lax.fori_loop(0, KF // FINE, body, 0)


def near_first(step, count):
    return jnp.where(step % 2 == 1, (step + 1) // 2, count - step // 2)


def far_first(step, count):
    away = count // 2 - (step + 1) // 2
    return jnp.where(step % 2 == 1, away, count - away)


def transform_kernel(lon, lat, count_hbm, block_hbm, stencil_hbm, frac_hbm, own_hbm, table_hbm, out_ref, *refs):
    (count_ref, block_ref, stencil_ref, frac_ref, own_ref, small) = refs[:6]
    (outbox, inbox, give, take, cells_ref, tiles, onehot, weight, departed, sectors, detour, plus, minus, table, total) = refs[6:21]
    (blocks, landed, wide, packs, bands) = refs[21:26]
    (fetch_sem, send_word, recv_word, send_value, recv_value, send_row, recv_row, detour_sem, onward_row) = refs[26:35]
    (send_block, recv_block, send_band, recv_band) = refs[35:]
    me_lon, me_lat = lax.axis_index("lon"), lax.axis_index("lat")
    rows = departed.shape[0]
    depth = blocks.shape[2]
    each = depth // lat
    chips = lon // 2
    me_chip, me_core = me_lon // 2, me_lon % 2
    tall = 8 if lat == 32 else lat
    flat = lat // tall
    quarter = (chips // 4, chips - chips // 4)

    barrier = pltpu.get_barrier_semaphore()

    def greet_lon(step, carry):
        peer = lax.rem(me_lon + step, lon)
        pl.semaphore_signal(barrier, inc=1, device_id={"lon": peer}, device_id_type=MESH)
        return carry

    def greet_lat(step, carry):
        peer = lax.rem(me_lat + step, lat)
        pl.semaphore_signal(barrier, inc=1, device_id={"lat": peer}, device_id_type=MESH)
        return carry

    lax.fori_loop(1, lon, greet_lon, 0)
    lax.fori_loop(1, lat, greet_lat, 0)
    pairs = (
        (own_hbm, own_ref),
        (count_hbm, count_ref),
        (block_hbm, block_ref),
        (stencil_hbm, stencil_ref),
        (frac_hbm, frac_ref),
        (table_hbm, small),
    )
    fetches = [pltpu.make_async_copy(src, dst, fetch_sem.at[k]) for k, (src, dst) in enumerate(pairs)]
    for fetch in fetches:
        fetch.start()
    fetches[0].wait()

    weight[:COLS, :] = own_ref[...].astype(jnp.float32)
    for cell in range(BLK):
        tiles[:BLOCKS, cell * 128 : (cell + 1) * 128] = weight[
            pl.ds(cell, BLOCKS, stride=BLK), :
        ].astype(jnp.bfloat16)
    tiles[BLOCKS:, :] = jnp.zeros((256 - BLOCKS, BLK * 128), jnp.bfloat16)
    for fetch in fetches[1:]:
        fetch.wait()
    first = count_ref[0]
    second = first + count_ref[1]
    order_requests(first, second, block_ref, stencil_ref, frac_ref, outbox, cells_ref)
    pl.semaphore_wait(barrier, lon + lat - 2)

    def beside(side):
        return lax.rem(me_lon + jnp.where(side == 0, lon - 1, 1), lon)

    def word_copy(side):
        return pltpu.make_async_remote_copy(
            src_ref=outbox.at[side],
            dst_ref=inbox.at[1 - side],
            send_sem=send_word.at[side],
            recv_sem=recv_word.at[1 - side],
            device_id={"lon": beside(side)},
            device_id_type=MESH,
        )

    def value_copy(side, piece):
        here = pl.ds(piece * (EDGE // 2), EDGE // 2)
        return pltpu.make_async_remote_copy(
            src_ref=give.at[side, here],
            dst_ref=take.at[1 - side, here],
            send_sem=send_value.at[side, piece],
            recv_sem=recv_value.at[1 - side, piece],
            device_id={"lon": beside(side)},
            device_id_type=MESH,
        )

    def weighted(base, count):
        here = pl.ds(pl.multiple_of(base, 128), count)
        values = jnp.zeros((count, 128), jnp.float32)
        for pair in range(BLK // 2):
            got = jnp.dot(
                onehot[here, :],
                tiles[:, pair * 256 : (pair + 1) * 256],
                preferred_element_type=jnp.float32,
            )
            scale = weight[here, :]
            values = values + scale[:, 2 * pair : 2 * pair + 1] * got[:, :128]
            values = values + scale[:, 2 * pair + 1 : 2 * pair + 2] * got[:, 128:]
        return values.astype(jnp.bfloat16).reshape(count // 128, 128, 128)

    for side in range(2):
        word_copy(side).start()
    middle = range(4, 20)
    decode(cells_ref[...], middle, 2 * CAP, onehot, weight)
    for side in (me_core, 1 - me_core):
        word_copy(1 - side).wait_recv()
        decode(inbox[side], range(EDGE), side * CAP, onehot, weight)
        for piece in range(2):
            rows_here = pl.ds(piece * (EDGE // 2), EDGE // 2)
            give[side, rows_here] = weighted(side * CAP + piece * (CAP // 2), CAP // 2)
            value_copy(side, piece).start()
    for piece in range(4):
        departed[4 + piece * 4 : 8 + piece * 4] = weighted(2 * CAP + piece * 512, 512)
    for side in range(2):
        for piece in range(2):
            value_copy(1 - side, piece).wait_recv()
    departed[:4] = take[0, :4]
    departed[20:] = take[1, 6:]
    for low, side, start in ((4, 0, 4), (14, 1, 0)):
        here = pl.ds(low, 6)
        departed[here] = (
            departed[here].astype(jnp.float32) + take[side, start : start + 6].astype(jnp.float32)
        ).astype(jnp.bfloat16)

    def slot_of(source):
        return sectors.at[source // 2, pl.ds(pl.multiple_of((source % 2) * 128, 128), 128), :]

    def row_copy(source, row, slot_send, slot_recv):
        return pltpu.make_async_remote_copy(
            src_ref=departed.at[row],
            dst_ref=slot_of(source),
            send_sem=send_row.at[slot_send],
            recv_sem=recv_row.at[slot_recv],
            device_id={"lon": row},
            device_id_type=MESH,
        )

    def row_detour(row, core):
        return pltpu.make_async_remote_copy(
            src_ref=departed.at[row],
            dst_ref=detour.at[core],
            send_sem=send_row.at[row],
            recv_sem=detour_sem.at[core],
            device_id={"lon": lax.rem(me_chip + quarter[core], chips) * 2 + me_core},
            device_id_type=MESH,
        )

    def row_onward(core):
        source = lax.rem(me_chip + chips - quarter[core], chips) * 2 + me_core
        return pltpu.make_async_remote_copy(
            src_ref=detour.at[core],
            dst_ref=slot_of(source),
            send_sem=onward_row.at[core],
            recv_sem=recv_row.at[source],
            device_id={"lon": lax.rem(me_chip + quarter[core], chips) * 2 + core},
            device_id_type=MESH,
        )

    def send_rows(step, carry):
        chip = lax.rem(me_chip + far_first(step, chips), chips)
        for core in range(2):
            row = chip * 2 + core

            @pl.when(step == 0)
            def _():
                row_detour(row, core).start()

            @pl.when(jnp.logical_and(step > 0, row != me_lon))
            def _():
                row_copy(me_lon, row, row, me_lon).start()

        return carry

    lax.fori_loop(0, chips, send_rows, 0)
    slot_of(me_lon)[...] = departed[me_lon]
    fill_table(small, plus, minus, table)
    total[...] = jnp.zeros_like(total)
    for core in range(2):
        row_detour(0, core).wait_recv()
        row_onward(core).start()

    def accumulate(step, carry):
        chip = lax.rem(me_chip + near_first(step, chips), chips)
        for core in range(2):
            source = chip * 2 + core

            @pl.when(source != me_lon)
            def _():
                row_copy(source, 0, source, source).wait_recv()

        for part in range(3):
            here = slice(part * (KF // 3), (part + 1) * (KF // 3))
            total[here, :] += jnp.dot(table[chip, here, :], sectors[chip], preferred_element_type=jnp.float32)
        return carry

    lax.fori_loop(0, chips, accumulate, 0)

    def block_copy(parity, source, block, slot_send, slot_recv):
        return pltpu.make_async_remote_copy(
            src_ref=blocks.at[parity, block],
            dst_ref=landed.at[parity, source],
            send_sem=send_block.at[parity, slot_send],
            recv_sem=recv_block.at[parity, slot_recv],
            device_id={"lon": block},
            device_id_type=MESH,
        )

    blocks[...] = total[...].astype(jnp.bfloat16).reshape(blocks.shape)
    for parity in range(2):

        def send_blocks(step, carry):
            chip = lax.rem(me_chip + far_first(step, chips), chips)
            for core in range(2):
                block = chip * 2 + core

                @pl.when(block != me_lon)
                def _():
                    block_copy(parity, me_lon, block, block, me_lon).start()

            return carry

        lax.fori_loop(0, chips, send_blocks, 0)

    def band_copy(parity, source, target, slot_send, slot_recv):
        return pltpu.make_async_remote_copy(
            src_ref=packs.at[parity, target],
            dst_ref=bands.at[parity, source],
            send_sem=send_band.at[parity, slot_send],
            recv_sem=recv_band.at[parity, slot_recv],
            device_id={"lat": target},
            device_id_type=MESH,
        )

    for parity in range(2):
        wide[parity, pl.ds(pl.multiple_of(me_lon * depth, depth), depth), :] = blocks[parity, me_lon].astype(jnp.float32)

        def widen(step, carry):
            chip = lax.rem(me_chip + near_first(step, chips), chips)
            for core in range(2):
                source = chip * 2 + core

                @pl.when(source != me_lon)
                def _():
                    block_copy(parity, source, 0, source, source).wait_recv()
                    here = pl.ds(pl.multiple_of(source * depth, depth), depth)
                    wide[parity, here, :] = landed[parity, source].astype(jnp.float32)

            return carry

        lax.fori_loop(0, chips, widen, 0)

        def send_bands(step, carry):
            column = lax.rem(me_lat % flat + far_first(step // tall, flat), flat)
            target = lax.rem(me_lat // flat + far_first(step % tall, tall), tall) * flat + column
            picked = [wide[parity, pl.ds(target * each + k, lon, stride=depth), :] for k in range(each)]
            packs[parity, target] = jnp.concatenate(picked, axis=0).astype(jnp.bfloat16)

            @pl.when(target != me_lat)
            def _():
                band_copy(parity, me_lat, target, target, me_lat).start()

            return carry

        lax.fori_loop(0, lat, send_bands, 0)
        bands[parity, me_lat] = packs[parity, me_lat]

    for side in range(2):
        word_copy(side).wait_send()
        for piece in range(2):
            value_copy(side, piece).wait_send()
        row_onward(side).wait_send()

    def finish_rows(step, carry):
        peer = lax.rem(me_lon + step, lon)
        row_copy(me_lon, peer, peer, me_lon).wait_send()
        for parity in range(2):
            block_copy(parity, me_lon, peer, peer, me_lon).wait_send()
        return carry

    lax.fori_loop(1, lon, finish_rows, 0)

    def finish_bands(step, carry):
        peer = lax.rem(me_lat + step, lat)
        for parity in range(2):
            band_copy(parity, peer, 0, peer, peer).wait_recv()
            band_copy(parity, me_lat, peer, peer, me_lat).wait_send()
        return carry

    lax.fori_loop(1, lat, finish_bands, 0)
    out_ref[...] = bands[...]


def transform(lon, lat, count, block, stencil, frac, own):
    depth = KF // lon // 2
    band = (2, lat, depth // lat * lon, 128)
    small = small_tables()
    return pl.pallas_call(
        functools.partial(transform_kernel, lon, lat),
        out_shape=jax.ShapeDtypeStruct(band, jnp.bfloat16),
        in_specs=[pl.BlockSpec(memory_space=pltpu.HBM)] * 6,
        out_specs=pl.BlockSpec(memory_space=pltpu.VMEM),
        scratch_shapes=[
            pltpu.SMEM((3,), jnp.int32),
            pltpu.VMEM(block.shape, jnp.int32),
            pltpu.VMEM(stencil.shape, jnp.int32),
            pltpu.VMEM(frac.shape, jnp.int32),
            pltpu.VMEM((COLS, 128), jnp.bfloat16),
            pltpu.VMEM(small.shape, jnp.float32),
            pltpu.VMEM((2, COLS // 128, 128), jnp.int32),
            pltpu.VMEM((2, COLS // 128, 128), jnp.int32),
            pltpu.VMEM((2, EDGE, 128, 128), jnp.bfloat16),
            pltpu.VMEM((2, EDGE, 128, 128), jnp.bfloat16),
            pltpu.VMEM((COLS // 128, 128), jnp.int32),
            pltpu.VMEM((256, BLK * 128), jnp.bfloat16),
            pltpu.VMEM((2 * CAP + 2048, 256), jnp.bfloat16),
            pltpu.VMEM((2 * CAP + 2048, 128), jnp.float32),
            pltpu.VMEM((COLS // 128, 128, 128), jnp.bfloat16),
            pltpu.VMEM((lon // 2, 256, 128), jnp.bfloat16),
            pltpu.VMEM((2, 128, 128), jnp.bfloat16),
            pltpu.VMEM((FINE, NLON), jnp.float32),
            pltpu.VMEM((FINE, NLON), jnp.float32),
            pltpu.VMEM((NLON // 256, KF, 256), jnp.bfloat16),
            pltpu.VMEM((KF, 128), jnp.float32),
            pltpu.VMEM((2, lon, depth, 128), jnp.bfloat16),
            pltpu.VMEM((2, lon, depth, 128), jnp.bfloat16),
            pltpu.VMEM((2, lon * depth, 128), jnp.float32),
            pltpu.VMEM(band, jnp.bfloat16),
            pltpu.VMEM(band, jnp.bfloat16),
            pltpu.SemaphoreType.DMA((6,)),
            pltpu.SemaphoreType.DMA((2,)),
            pltpu.SemaphoreType.DMA((2,)),
            pltpu.SemaphoreType.DMA((2, 2)),
            pltpu.SemaphoreType.DMA((2, 2)),
            pltpu.SemaphoreType.DMA((lon,)),
            pltpu.SemaphoreType.DMA((lon,)),
            pltpu.SemaphoreType.DMA((2,)),
            pltpu.SemaphoreType.DMA((2,)),
            pltpu.SemaphoreType.DMA((2, lon)),
            pltpu.SemaphoreType.DMA((2, lon)),
            pltpu.SemaphoreType.DMA((2, lat)),
            pltpu.SemaphoreType.DMA((2, lat)),
        ],
        compiler_params=pltpu.CompilerParams(
            vmem_limit_bytes=62976 << 10, collective_id=0, has_side_effects=True
        ),
        name="transform",
    )(count, block, stencil, frac, own, small)


def gathered_bands(fields, req_block, req_stencil, req_frac, req_count):
    lon = lax.axis_size("lon")
    lat = lax.axis_size("lat")
    block = req_block[0, 0].reshape(3, 1, CAP)
    bands = transform(
        lon, lat, req_count[0, 0], block, req_stencil[0, 0], req_frac[0, 0], fields.reshape(COLS, 128)
    )
    half = KF // lon // lat // 2
    bands = bands.reshape(2, lat, half, lon, 128).transpose(2, 0, 1, 3, 4)
    return bands.reshape(2 * half, lat * lon, 128)


def local(fields, req_block, req_stencil, req_frac, req_count, legendre):
    gathered = gathered_bands(fields, req_block, req_stencil, req_frac, req_count)
    projected = jnp.einsum("kyn,kyc->knc", legendre, gathered, preferred_element_type=jnp.float32)
    degree = jnp.arange(NN, dtype=jnp.float32)
    factor = 1.0 / (1.0 + 4.0 * degree * (degree + 1.0) / (NN * (NN + 1)))
    return projected * factor[None, :, None]


def solution(mesh):
    return jax.shard_map(
        local,
        mesh=mesh,
        in_specs=(
            P("lat", "lon", None),
            P("lat", "lon", None, None),
            P("lat", "lon", None, None, None),
            P("lat", "lon", None, None, None),
            P("lat", "lon", None),
            P(("lon", "lat"), None, None),
        ),
        out_specs=P(("lon", "lat"), None, None),
        check_vma=False,
    )
```

```python
import functools
import math

import jax
import jax.numpy as jnp
import numpy as np
from jax import lax
from jax.experimental import pallas as pl
from jax.experimental.pallas import tpu as pltpu
from jax.sharding import PartitionSpec as P

KF = 1536
NN = 768
BLK = 16
FRAC = 16
COLS = 3072
CAP = 1280
NLON = 3072
BLOCKS = COLS // BLK
FINE = 96
CHUNK = 4
MESH = pl.DeviceIdType.MESH


def small_tables():
    unit = 2.0 * math.pi / NLON
    fine = np.concatenate([np.arange(0, FINE, 2), np.arange(1, FINE, 2)]).astype(np.int64)[:, None]
    lane = np.arange(128, dtype=np.int64)[None, :]
    scale = 1.0 / math.sqrt(NLON)
    near = unit * (fine * lane % NLON)
    plus = (np.cos(near) + np.sin(near)) * scale
    minus = (np.cos(near) - np.sin(near)) * scale
    far = unit * (fine * lane * 128 % NLON)
    coarse = unit * (np.arange(KF // FINE, dtype=np.int64)[:, None] * FINE * lane % NLON)
    tables = [plus, minus, np.cos(far), np.sin(far), np.cos(coarse), np.sin(coarse)]
    return np.concatenate(tables, axis=0).astype(np.float32)


def order_requests(first, second, block_ref, stencil_ref, frac_ref, cells_ref):
    lane = lax.broadcasted_iota(jnp.int32, (32, 128), 1)
    cell = lax.broadcasted_iota(jnp.int32, (32, 128), 0) * 128 + lane
    shift4 = 20 - 4 * lax.broadcasted_iota(jnp.int32, (4, CAP), 0)
    shift2 = 4 - 4 * lax.broadcasted_iota(jnp.int32, (2, CAP), 0)
    result = None
    for slot, start in ((0, None), (1, first), (2, second)):
        word = (
            lax.shift_left(block_ref[slot], jnp.full((1, CAP), 24, jnp.int32))
            + jnp.sum(lax.shift_left(stencil_ref[slot], shift4), axis=0, keepdims=True)
            + jnp.sum(lax.shift_left(frac_ref[slot], shift2), axis=0, keepdims=True)
        )
        pieces = [word[:, k * 128 : (k + 1) * 128] for k in range(CAP // 128)]
        pieces.append(jnp.zeros((32 - CAP // 128, 128), jnp.int32))
        placed = jnp.concatenate(pieces, axis=0)
        if start is None:
            result = placed
            continue
        moved = jnp.full((32, 128), start, jnp.int32)
        for bit in range(12):
            if bit < 7:
                turned = pltpu.roll(placed, 1 << bit, 1)
                turned = jnp.where(lane < (1 << bit), pltpu.roll(turned, 1, 0), turned)
            else:
                turned = pltpu.roll(placed, 1 << (bit - 7), 0)
            chosen = lax.shift_right_logical(moved, jnp.full((32, 128), bit, jnp.int32)) & 1
            placed = jnp.where(chosen == 1, turned, placed)
        result = jnp.where(cell < moved, result, placed)
    cells_ref[...] = result[: cells_ref.shape[0], :]


def decode(first, second, cells_ref, onehot_ref, weight_ref):
    rows = cells_ref.shape[0]
    columns = jnp.concatenate(
        [cells_ref[...], jnp.zeros((128 - rows, 128), jnp.int32)], axis=0
    ).T
    lane = lax.broadcasted_iota(jnp.int32, (128, 128), 1)
    sub = lax.broadcasted_iota(jnp.int32, (128, 128), 0)
    for row in range(rows):
        word = jnp.broadcast_to(columns[:, row : row + 1], (128, 128))
        block = lax.shift_right_logical(word, 24)
        edge = first if row < rows // 2 else second
        block = block + jnp.where(sub + row * 128 >= edge, BLOCKS, 0)
        here = pl.ds(row * 128, 128)
        for part in range(3):
            onehot_ref[here, part * 128 : (part + 1) * 128] = jnp.where(
                block == lane + part * 128, 1.0, 0.0
            ).astype(jnp.bfloat16)
        frac_lat = ((lax.shift_right_logical(word, 4) & 15).astype(jnp.float32) + 0.5) / FRAC
        frac_lon = ((word & 15).astype(jnp.float32) + 0.5) / FRAC
        corner = (
            (1.0 - frac_lat) * (1.0 - frac_lon),
            frac_lat * (1.0 - frac_lon),
            (1.0 - frac_lat) * frac_lon,
            frac_lat * frac_lon,
        )
        weight = jnp.zeros((128, 128), jnp.float32)
        for k in range(4):
            spot = lax.shift_right_logical(word, 20 - 4 * k) & 15
            weight = weight + jnp.where(spot == lane, corner[k], 0.0)
        weight_ref[here, :] = weight


def fill_table(small, plus, minus, table):
    near_plus, near_minus, far_cos, far_sin = [small.at[pl.ds(k * FINE, FINE)] for k in range(4)]
    coarse_cos, coarse_sin = [small.at[pl.ds(4 * FINE + k * (KF // FINE), KF // FINE)] for k in range(2)]
    for sector in range(NLON // 128):
        here = pl.ds(sector * 128, 128)
        turn_cos = far_cos[:, sector : sector + 1]
        turn_sin = far_sin[:, sector : sector + 1]
        plus[:, here] = turn_cos * near_plus[...] + turn_sin * near_minus[...]
        minus[:, here] = turn_cos * near_minus[...] - turn_sin * near_plus[...]

    def body(step, carry):
        cos = coarse_cos[pl.ds(step, 1), :]
        sin = coarse_sin[pl.ds(step, 1), :]
        for parity in range(2):
            here = slice(parity * (FINE // 2), (parity + 1) * (FINE // 2))
            rows = pl.ds(pl.multiple_of(step * (FINE // 2), FINE // 2) + parity * (KF // 2), FINE // 2)
            for sector in range(NLON // 128):
                lanes = slice(sector * 128, (sector + 1) * 128)
                table[sector // 2, rows, (sector % 2) * 128 : (sector % 2 + 1) * 128] = (
                    cos * plus[here, lanes] + sin * minus[here, lanes]
                ).astype(jnp.bfloat16)
        return carry

    lax.fori_loop(0, KF // FINE, body, 0)


def near_first(step, count):
    return jnp.where(step % 2 == 1, (step + 1) // 2, count - step // 2)


def far_first(step, count):
    away = count // 2 - (step + 1) // 2
    return jnp.where(step % 2 == 1, away, count - away)


def transform_kernel(lon, lat, count_hbm, block_hbm, stencil_hbm, frac_hbm, own_hbm, table_hbm, out_ref, *refs):
    (count_ref, block_ref, stencil_ref, frac_ref, own_ref, small) = refs[:6]
    (cells_ref, tiles, onehot, weight, departed, sectors, plus, minus, table, total) = refs[6:16]
    (blocks, landed, wide, packs, bands) = refs[16:21]
    (fetch_sem, send_tile, recv_tile, send_row, recv_row) = refs[21:26]
    (send_block, recv_block, send_band, recv_band) = refs[26:]
    me_lon, me_lat = lax.axis_index("lon"), lax.axis_index("lat")
    rows = departed.shape[0]
    depth = blocks.shape[2]
    each = depth // lat
    chips = lon // 2
    me_chip, me_core = me_lon // 2, me_lon % 2
    tall = 8 if lat == 32 else lat
    flat = lat // tall

    barrier = pltpu.get_barrier_semaphore()

    def greet_lon(step, carry):
        peer = lax.rem(me_lon + step, lon)
        pl.semaphore_signal(barrier, inc=1, device_id={"lon": peer}, device_id_type=MESH)
        return carry

    def greet_lat(step, carry):
        peer = lax.rem(me_lat + step, lat)
        pl.semaphore_signal(barrier, inc=1, device_id={"lat": peer}, device_id_type=MESH)
        return carry

    lax.fori_loop(1, lon, greet_lon, 0)
    lax.fori_loop(1, lat, greet_lat, 0)
    pairs = (
        (own_hbm, own_ref),
        (count_hbm, count_ref),
        (block_hbm, block_ref),
        (stencil_hbm, stencil_ref),
        (frac_hbm, frac_ref),
        (table_hbm, small),
    )
    fetches = [pltpu.make_async_copy(src, dst, fetch_sem.at[k]) for k, (src, dst) in enumerate(pairs)]
    for fetch in fetches:
        fetch.start()
    fetches[0].wait()

    weight[...] = own_ref[...].astype(jnp.float32)
    for cell in range(BLK):
        tiles[BLOCKS : 2 * BLOCKS, cell * 128 : (cell + 1) * 128] = weight[
            pl.ds(cell, BLOCKS, stride=BLK), :
        ].astype(jnp.bfloat16)
    pl.semaphore_wait(barrier, lon + lat - 2)

    def tile_copy(side):
        return pltpu.make_async_remote_copy(
            src_ref=tiles.at[pl.ds(BLOCKS, BLOCKS)],
            dst_ref=tiles.at[pl.ds(2 * BLOCKS * side, BLOCKS)],
            send_sem=send_tile.at[side],
            recv_sem=recv_tile.at[side],
            device_id={"lon": lax.rem(me_lon + jnp.where(side == 0, 1, lon - 1), lon)},
            device_id_type=MESH,
        )

    tile_copy(me_core).start()
    tile_copy(1 - me_core).start()
    for fetch in fetches[1:]:
        fetch.wait()
    first = count_ref[0]
    second = first + count_ref[1]
    order_requests(first, second, block_ref, stencil_ref, frac_ref, cells_ref)
    decode(first, second, cells_ref, onehot, weight)

    def slot_of(source):
        return sectors.at[source // 2, pl.ds(pl.multiple_of((source % 2) * 128, 128), 128), :]

    def row_copy(source, row, slot_send, slot_recv):
        return pltpu.make_async_remote_copy(
            src_ref=departed.at[row],
            dst_ref=slot_of(source),
            send_sem=send_row.at[slot_send],
            recv_sem=recv_row.at[slot_recv],
            device_id={"lon": row},
            device_id_type=MESH,
        )

    parts = rows // CHUNK

    def interpolate(part, carry):
        low = pl.multiple_of(jnp.where(part < parts // 2, 0, BLOCKS), BLOCKS)
        here = pl.ds(pl.multiple_of(part * CHUNK * 128, CHUNK * 128), CHUNK * 128)
        values = jnp.zeros((CHUNK * 128, 128), jnp.float32)
        for pair in range(BLK // 2):
            got = jnp.dot(
                onehot[here, :],
                tiles[pl.ds(low, 2 * BLOCKS), pair * 256 : (pair + 1) * 256],
                preferred_element_type=jnp.float32,
            )
            scale = weight[here, :]
            values = values + scale[:, 2 * pair : 2 * pair + 1] * got[:, :128]
            values = values + scale[:, 2 * pair + 1 : 2 * pair + 2] * got[:, 128:]
        departed[pl.ds(part * CHUNK, CHUNK)] = values.astype(jnp.bfloat16).reshape(CHUNK, 128, 128)

        def send_rows(pair, inner):
            chip = part * (CHUNK // 2) + pair
            for core in range(2):
                row = chip * 2 + core

                @pl.when(row != me_lon)
                def _():
                    row_copy(me_lon, row, row, me_lon).start()

            return inner

        lax.fori_loop(0, CHUNK // 2, send_rows, 0)
        return carry

    for turn in range(2):
        half = 1 - me_core if turn == 0 else me_core
        tile_copy(half).wait_recv()
        lax.fori_loop(half * (parts // 2), (half + 1) * (parts // 2), interpolate, 0)
    slot_of(me_lon)[...] = departed[me_lon]
    fill_table(small, plus, minus, table)
    total[...] = jnp.zeros_like(total)

    def accumulate(step, carry):
        chip = lax.rem(me_chip + near_first(step, chips), chips)
        for core in range(2):
            source = chip * 2 + core

            @pl.when(source != me_lon)
            def _():
                row_copy(source, 0, source, source).wait_recv()

        for part in range(3):
            here = slice(part * (KF // 3), (part + 1) * (KF // 3))
            total[here, :] += jnp.dot(table[chip, here, :], sectors[chip], preferred_element_type=jnp.float32)
        return carry

    lax.fori_loop(0, chips, accumulate, 0)

    def block_copy(parity, source, block, slot_send, slot_recv):
        return pltpu.make_async_remote_copy(
            src_ref=blocks.at[parity, block],
            dst_ref=landed.at[parity, source],
            send_sem=send_block.at[parity, slot_send],
            recv_sem=recv_block.at[parity, slot_recv],
            device_id={"lon": block},
            device_id_type=MESH,
        )

    blocks[...] = total[...].astype(jnp.bfloat16).reshape(blocks.shape)
    for parity in range(2):

        def send_blocks(step, carry):
            chip = lax.rem(me_chip + far_first(step, chips), chips)
            for core in range(2):
                block = chip * 2 + core

                @pl.when(block != me_lon)
                def _():
                    block_copy(parity, me_lon, block, block, me_lon).start()

            return carry

        lax.fori_loop(0, chips, send_blocks, 0)
    def band_copy(parity, source, target, slot_send, slot_recv):
        return pltpu.make_async_remote_copy(
            src_ref=packs.at[parity, target],
            dst_ref=bands.at[parity, source],
            send_sem=send_band.at[parity, slot_send],
            recv_sem=recv_band.at[parity, slot_recv],
            device_id={"lat": target},
            device_id_type=MESH,
        )

    for parity in range(2):
        wide[parity, pl.ds(pl.multiple_of(me_lon * depth, depth), depth), :] = blocks[parity, me_lon].astype(jnp.float32)

        def widen(step, carry):
            chip = lax.rem(me_chip + near_first(step, chips), chips)
            for core in range(2):
                source = chip * 2 + core

                @pl.when(source != me_lon)
                def _():
                    block_copy(parity, source, 0, source, source).wait_recv()
                    here = pl.ds(pl.multiple_of(source * depth, depth), depth)
                    wide[parity, here, :] = landed[parity, source].astype(jnp.float32)

            return carry

        lax.fori_loop(0, chips, widen, 0)

        def send_bands(step, carry):
            column = lax.rem(me_lat % flat + far_first(step // tall, flat), flat)
            target = lax.rem(me_lat // flat + far_first(step % tall, tall), tall) * flat + column
            picked = [wide[parity, pl.ds(target * each + k, lon, stride=depth), :] for k in range(each)]
            packs[parity, target] = jnp.concatenate(picked, axis=0).astype(jnp.bfloat16)

            @pl.when(target != me_lat)
            def _():
                band_copy(parity, me_lat, target, target, me_lat).start()

            return carry

        lax.fori_loop(0, lat, send_bands, 0)
        bands[parity, me_lat] = packs[parity, me_lat]

    for side in range(2):
        tile_copy(side).wait_send()

    def finish_rows(step, carry):
        peer = lax.rem(me_lon + step, lon)
        row_copy(me_lon, peer, peer, me_lon).wait_send()
        for parity in range(2):
            block_copy(parity, me_lon, peer, peer, me_lon).wait_send()
        return carry

    lax.fori_loop(1, lon, finish_rows, 0)

    def finish_bands(step, carry):
        peer = lax.rem(me_lat + step, lat)
        for parity in range(2):
            band_copy(parity, peer, 0, peer, peer).wait_recv()
            band_copy(parity, me_lat, peer, peer, me_lat).wait_send()
        return carry

    lax.fori_loop(1, lat, finish_bands, 0)
    out_ref[...] = bands[...]


def transform(lon, lat, count, block, stencil, frac, own):
    depth = KF // lon // 2
    band = (2, lat, depth // lat * lon, 128)
    small = small_tables()
    return pl.pallas_call(
        functools.partial(transform_kernel, lon, lat),
        out_shape=jax.ShapeDtypeStruct(band, jnp.bfloat16),
        in_specs=[pl.BlockSpec(memory_space=pltpu.HBM)] * 6,
        out_specs=pl.BlockSpec(memory_space=pltpu.VMEM),
        scratch_shapes=[
            pltpu.SMEM((3,), jnp.int32),
            pltpu.VMEM(block.shape, jnp.int32),
            pltpu.VMEM(stencil.shape, jnp.int32),
            pltpu.VMEM(frac.shape, jnp.int32),
            pltpu.VMEM((COLS, 128), jnp.bfloat16),
            pltpu.VMEM(small.shape, jnp.float32),
            pltpu.VMEM((COLS // 128, 128), jnp.int32),
            pltpu.VMEM((3 * BLOCKS, BLK * 128), jnp.bfloat16),
            pltpu.VMEM((COLS, 2 * BLOCKS), jnp.bfloat16),
            pltpu.VMEM((COLS, 128), jnp.float32),
            pltpu.VMEM((COLS // 128, 128, 128), jnp.bfloat16),
            pltpu.VMEM((lon // 2, 256, 128), jnp.bfloat16),
            pltpu.VMEM((FINE, NLON), jnp.float32),
            pltpu.VMEM((FINE, NLON), jnp.float32),
            pltpu.VMEM((NLON // 256, KF, 256), jnp.bfloat16),
            pltpu.VMEM((KF, 128), jnp.float32),
            pltpu.VMEM((2, lon, depth, 128), jnp.bfloat16),
            pltpu.VMEM((2, lon, depth, 128), jnp.bfloat16),
            pltpu.VMEM((2, lon * depth, 128), jnp.float32),
            pltpu.VMEM(band, jnp.bfloat16),
            pltpu.VMEM(band, jnp.bfloat16),
            pltpu.SemaphoreType.DMA((6,)),
            pltpu.SemaphoreType.DMA((2,)),
            pltpu.SemaphoreType.DMA((2,)),
            pltpu.SemaphoreType.DMA((lon,)),
            pltpu.SemaphoreType.DMA((lon,)),
            pltpu.SemaphoreType.DMA((2, lon)),
            pltpu.SemaphoreType.DMA((2, lon)),
            pltpu.SemaphoreType.DMA((2, lat)),
            pltpu.SemaphoreType.DMA((2, lat)),
        ],
        compiler_params=pltpu.CompilerParams(
            vmem_limit_bytes=62976 << 10, collective_id=0, has_side_effects=True
        ),
        name="transform",
    )(count, block, stencil, frac, own, small)


def gathered_bands(fields, req_block, req_stencil, req_frac, req_count):
    lon = lax.axis_size("lon")
    lat = lax.axis_size("lat")
    block = req_block[0, 0].reshape(3, 1, CAP)
    bands = transform(
        lon, lat, req_count[0, 0], block, req_stencil[0, 0], req_frac[0, 0], fields.reshape(COLS, 128)
    )
    half = KF // lon // lat // 2
    bands = bands.reshape(2, lat, half, lon, 128).transpose(2, 0, 1, 3, 4)
    return bands.reshape(2 * half, lat * lon, 128)


def local(fields, req_block, req_stencil, req_frac, req_count, legendre):
    gathered = gathered_bands(fields, req_block, req_stencil, req_frac, req_count)
    projected = jnp.einsum("kyn,kyc->knc", legendre, gathered, preferred_element_type=jnp.float32)
    degree = jnp.arange(NN, dtype=jnp.float32)
    factor = 1.0 / (1.0 + 4.0 * degree * (degree + 1.0) / (NN * (NN + 1)))
    return projected * factor[None, :, None]


def solution(mesh):
    return jax.shard_map(
        local,
        mesh=mesh,
        in_specs=(
            P("lat", "lon", None),
            P("lat", "lon", None, None),
            P("lat", "lon", None, None, None),
            P("lat", "lon", None, None, None),
            P("lat", "lon", None),
            P(("lon", "lat"), None, None),
        ),
        out_specs=P(("lon", "lat"), None, None),
        check_vma=False,
    )
```
